32 devices in a mesh: section: 4 (over y, x), dp: 8 (over z, core).
Axes of the slice: x: 2, y: 2, z: 4, core: 2. Of those that a mesh axis runs over, the one named last changes fastest.
Arguments:
- hidden_in: bfloat16 [4, 8, 256, 2048], P('section', 'dp'), may hold values from -6 to 6
- grad_out: bfloat16 [8, 256, 2048], P('dp'), may hold values from -6 to 6
- encoder_out: bfloat16 [8, 256, 2048], P('dp', 'section'), may hold values from -6 to 6
- enc_valid: int32 [8, 256], P('dp', 'section'), may hold values from 0 to 1, as said below
- norm_gain: bfloat16 [4, 2048], P('section'), may hold values from 0.099609375 to 1.8984375
- w_query: bfloat16 [4, 2048, 2048], P('section', 'dp'), may hold values from -0.015625 to 0.015625
- w_key: bfloat16 [4, 2048, 2048], P('section', 'dp'), may hold values from -0.125 to 0.125
- w_value: bfloat16 [4, 2048, 2048], P('section', 'dp'), may hold values from -0.125 to 0.125
- w_out: bfloat16 [4, 2048, 2048], P('section', 'dp'), may hold values from -0.875 to 0.875
Outputs:
- grad_in: bfloat16 [4, 8, 256, 2048], P('section', 'dp')
- grad_encoder: bfloat16 [8, 256, 2048], P('dp', 'section')
The draws below stay inside these ranges and needn't reach their ends.
Inputs may be any that keep to these rules, and one draw needn't show every extreme that they name: `enc_valid`: each row is 1 on a prefix of 128 or more positions and 0 after it.
All inputs are finite; a program needn't handle non-finite values.
Results may differ from the reference program's by a relative error of at most 0.04.
Values may be sent and summed in bfloat16 or wider, within the bound.
No kernel may reach another device: no remote copies, remote signals or barrier semaphores. Data moves between devices by JAX's collectives and lax.ppermute only.
A program may use at most 192 MiB of HBM per device.

```python
import jax
import jax.numpy as jnp
from jax import lax

D = 2048
HEAD = 64
DEC_LEN = 256
ENC_LEN = 256
INNER = 2048
SEQS = 8
SECTIONS = 4


def draw_enc_valid(key, part):
    lengths = jax.random.randint(key, (SEQS,), ENC_LEN // 2, ENC_LEN + 1)
    lengths = lengths.at[0].set(ENC_LEN // 2).at[SEQS - 1].set(ENC_LEN)
    positions = jnp.arange(ENC_LEN, dtype=jnp.int32)
    return (positions[None, :] < lengths[:, None]).astype(jnp.int32)


def shard_levels(key, extent, cuts, smallest, high):
    def one(axis_at, shards_of):
        steps = jax.random.uniform(jax.random.fold_in(jax.random.fold_in(key, 6), axis_at), (shards_of,), jnp.float32, smallest / len(cuts), high / len(cuts))
        return jnp.repeat(jnp.exp(steps), extent[axis_at] // shards_of).reshape((-1,) + (1,) * (len(extent) - axis_at - 1))

    gain = one(*cuts[0])
    for cut in cuts[1:]:
        gain = gain * one(*cut)
    return gain


def normal_values(own_key, dims, deviation, bound, shards=(), held_as=jnp.bfloat16):
    array = deviation * jax.random.normal(own_key, dims, jnp.float32)
    if shards:
        array = array * shard_levels(own_key, dims, shards, -0.22, 0.18)
    return jnp.clip(array, -bound, bound).astype(held_as)


def setup_inputs(seed: int = 0) -> dict:
    arg_keys = jax.random.split(jax.random.key(seed), 10)
    hidden_in = normal_values(arg_keys[0], (SECTIONS, SEQS, DEC_LEN, D), 1.0, 6.0, ((0, 4), (1, 8)))
    grad_out = normal_values(arg_keys[1], (SEQS, DEC_LEN, D), 1.0, 6.0, ((0, 8),))
    encoder_out = normal_values(arg_keys[2], (SEQS, ENC_LEN, D), 1.0, 6.0, ((0, 8), (1, 4)))
    enc_valid = draw_enc_valid(jax.random.fold_in(arg_keys[9], 71), 0)
    norm_gain = jnp.clip(1.0 + 0.18 * jax.random.normal(arg_keys[4], (SECTIONS, D), jnp.float32), 0.099609375, 1.8984375).astype(jnp.bfloat16)
    w_query = normal_values(arg_keys[5], (SECTIONS, D, INNER), (D * HEAD) ** -0.5, 0.015625, ((0, 4), (1, 8)))
    w_key = normal_values(arg_keys[6], (SECTIONS, D, INNER), D ** -0.5, 0.125, ((0, 4), (1, 8)))
    w_value = normal_values(arg_keys[7], (SECTIONS, D, INNER), D ** -0.5, 0.125, ((0, 4), (1, 8)))
    w_out = normal_values(arg_keys[8], (SECTIONS, INNER, D), (6 * INNER // ENC_LEN) ** -0.5, 0.875, ((0, 4), (1, 8)))
    return dict(hidden_in=hidden_in, grad_out=grad_out, encoder_out=encoder_out, enc_valid=enc_valid, norm_gain=norm_gain, w_query=w_query, w_key=w_key, w_value=w_value, w_out=w_out)


def forward_section(inputs, gain_row, query_weight, key_weight, value_weight, encoded, valid_keys):
    seq_count, dec_rows, width = inputs.shape
    enc_rows = encoded.shape[1]
    inner_width = query_weight.shape[1]
    head_count = inner_width // HEAD
    in_float = inputs.astype(jnp.float32)
    inv_rms = lax.rsqrt(lax.optimization_barrier(jnp.mean(in_float * in_float, axis=2, keepdims=True)) + 1e-06)
    normed = (in_float * inv_rms * gain_row.astype(jnp.float32)).astype(jnp.bfloat16)
    queries = jnp.dot(normed.reshape(-1, width), query_weight, preferred_element_type=jnp.float32).astype(jnp.bfloat16)
    queries = queries.reshape(seq_count, dec_rows, head_count, HEAD)
    keys_all = jnp.dot(encoded.reshape(-1, width), key_weight, preferred_element_type=jnp.float32).astype(jnp.bfloat16)
    keys_all = keys_all.reshape(seq_count, enc_rows, head_count, HEAD)
    values_all = jnp.dot(encoded.reshape(-1, width), value_weight, preferred_element_type=jnp.float32).astype(jnp.bfloat16)
    values_all = values_all.reshape(seq_count, enc_rows, head_count, HEAD)
    scores = jnp.einsum('slhd,sehd->shle', queries.astype(jnp.float32), keys_all.astype(jnp.float32))
    raw = jnp.exp(scores) * valid_keys.astype(jnp.float32)[:, None, None, :]
    attn_prob = raw / lax.optimization_barrier(jnp.sum(raw, axis=3, keepdims=True))
    return (in_float, inv_rms, queries, keys_all, values_all, attn_prob)

def backward_section(grad_y, saved, gain_row, query_weight, out_weight):
    in_float, inv_rms, queries, keys_all, values_all, attn_prob = saved
    seq_count, dec_rows, width = grad_y.shape
    head_count = queries.shape[2]
    enc_rows = keys_all.shape[1]
    grad_attn = jnp.dot(grad_y.reshape(-1, width), out_weight.T, preferred_element_type=jnp.float32).astype(jnp.bfloat16)
    grad_attn = grad_attn.reshape(seq_count, dec_rows, head_count, HEAD)
    grad_prob = jnp.einsum('slhd,sehd->shle', grad_attn.astype(jnp.float32), values_all.astype(jnp.float32))
    inner_sum = lax.optimization_barrier(jnp.sum(attn_prob * grad_prob, axis=3, keepdims=True))
    grad_scores = (attn_prob * (grad_prob - inner_sum)).astype(jnp.bfloat16)
    prob_half = attn_prob.astype(jnp.bfloat16)
    grad_query = jnp.einsum('shle,sehd->slhd', grad_scores.astype(jnp.float32), keys_all.astype(jnp.float32)).astype(jnp.bfloat16)
    grad_key = jnp.einsum('shle,slhd->sehd', grad_scores.astype(jnp.float32), queries.astype(jnp.float32)).astype(jnp.bfloat16)
    grad_value = jnp.einsum('shle,slhd->sehd', prob_half.astype(jnp.float32), grad_attn.astype(jnp.float32)).astype(jnp.bfloat16)
    grad_normed = jnp.dot(grad_query.reshape(seq_count * dec_rows, -1), query_weight.T, preferred_element_type=jnp.float32)
    grad_normed = grad_normed.reshape(seq_count, dec_rows, width)
    scaled_grad = gain_row.astype(jnp.float32) * grad_normed
    branch = inv_rms * scaled_grad - in_float * inv_rms * inv_rms * inv_rms * lax.optimization_barrier(jnp.mean(in_float * scaled_grad, axis=2, keepdims=True))
    grad_input = (grad_y.astype(jnp.float32) + branch).astype(jnp.bfloat16)
    return (grad_input, grad_key.reshape(seq_count * enc_rows, -1), grad_value.reshape(seq_count * enc_rows, -1))

def reference(hidden_in, grad_out, encoder_out, enc_valid, norm_gain, w_query, w_key, w_value, w_out):
    grad_now = grad_out
    grad_list = []
    enc_total = jnp.zeros((SEQS * ENC_LEN, D), jnp.float32)
    for section_index in reversed(range(SECTIONS)):
        saved = forward_section(hidden_in[section_index], norm_gain[section_index], w_query[section_index], w_key[section_index], w_value[section_index], encoder_out, enc_valid)
        grad_now, grad_key, grad_value = backward_section(grad_now, saved, norm_gain[section_index], w_query[section_index], w_out[section_index])
        grad_list.insert(0, grad_now)
        enc_total = enc_total + jnp.dot(grad_key, w_key[section_index].T, preferred_element_type=jnp.float32)
        enc_total = enc_total + jnp.dot(grad_value, w_value[section_index].T, preferred_element_type=jnp.float32)
    grad_encoder = enc_total.reshape(SEQS, ENC_LEN, D).astype(jnp.bfloat16)
    return (jnp.stack(grad_list), grad_encoder)
```

```python
import functools

import jax
import jax.numpy as jnp
from jax import lax
from jax.experimental import pallas as pl
from jax.experimental.pallas import tpu as pltpu
from jax.sharding import PartitionSpec as P

HEAD = 64


def from_behind(array, axis, by):
    length = lax.axis_size(axis)
    pairs = [(i, i + by) for i in range(length) if 0 <= i + by < length]
    return lax.ppermute(array, axis, pairs)


def times_transposed(left_side, right_side):
    return lax.dot_general(
        left_side, right_side, (((1,), (1,)), ((), ())), preferred_element_type=jnp.float32
    )


def project_keys(encoded, key_weight, value_weight):
    keys_all = jnp.dot(encoded, key_weight, preferred_element_type=jnp.float32).astype(jnp.bfloat16)
    values_all = jnp.dot(encoded, value_weight, preferred_element_type=jnp.float32).astype(
        jnp.bfloat16
    )
    return (keys_all, values_all)


def relay_device(
    hidden_in, grad_out, encoder_out, enc_valid, norm_gain, w_query, w_key, w_value, w_out
):
    section_count = lax.axis_size("section")
    my_section = lax.axis_index("section")
    valid_half = enc_valid.astype(jnp.bfloat16)
    encoded_all, valid_all = (
        lax.all_gather(encoder_out, "section", axis=1, tiled=True),
        lax.all_gather(valid_half, "section", axis=1, tiled=True),
    )
    encoded = encoded_all[0]
    valid_keys = valid_all[0].astype(jnp.float32)
    query_full, key_full, value_full, out_full = (
        lax.all_gather(w_query, "dp", axis=1, tiled=True),
        lax.all_gather(w_key, "dp", axis=1, tiled=True),
        lax.all_gather(w_value, "dp", axis=1, tiled=True),
        lax.all_gather(w_out, "dp", axis=1, tiled=True),
    )
    keys_all, values_all = project_keys(encoded, key_full[0], value_full[0])
    query_weight = query_full[0]
    key_weight = key_full[0]
    value_weight = value_full[0]
    out_weight = out_full[0]
    dec_rows, width = (hidden_in.shape[2], hidden_in.shape[3])
    enc_rows = encoded.shape[0]
    inner_width = query_weight.shape[1]
    head_count = inner_width // HEAD
    in_float = hidden_in[0, 0].astype(jnp.float32)
    gain_row = norm_gain[0].astype(jnp.float32)
    inv_rms = lax.rsqrt(jnp.mean(in_float * in_float, axis=1, keepdims=True) + 1e-06)
    normed = (in_float * inv_rms * gain_row).astype(jnp.bfloat16)
    queries = jnp.dot(normed, query_weight, preferred_element_type=jnp.float32).astype(jnp.bfloat16)
    query_heads = queries.reshape(dec_rows, head_count, HEAD)
    key_heads = keys_all.reshape(enc_rows, head_count, HEAD)
    value_heads = values_all.reshape(enc_rows, head_count, HEAD)
    scores = jnp.einsum("lhd,ehd->hle", query_heads, key_heads, preferred_element_type=jnp.float32)
    raw = jnp.exp(scores) * valid_keys[None, None, :]
    attn_prob = raw / jnp.sum(raw, axis=2, keepdims=True)
    prob_half = attn_prob.astype(jnp.bfloat16)

    def backward_step(grad_y):
        grad_attn = times_transposed(grad_y, out_weight).astype(jnp.bfloat16)
        attn_heads = grad_attn.reshape(dec_rows, head_count, HEAD)
        grad_prob = jnp.einsum(
            "lhd,ehd->hle", attn_heads, value_heads, preferred_element_type=jnp.float32
        )
        inner_sum = jnp.sum(attn_prob * grad_prob, axis=2, keepdims=True)
        grad_scores = (attn_prob * (grad_prob - inner_sum)).astype(jnp.bfloat16)
        grad_query = jnp.einsum(
            "hle,ehd->lhd", grad_scores, key_heads, preferred_element_type=jnp.float32
        ).astype(jnp.bfloat16)
        grad_key = jnp.einsum(
            "hle,lhd->ehd", grad_scores, query_heads, preferred_element_type=jnp.float32
        ).astype(jnp.bfloat16)
        grad_value = jnp.einsum(
            "hle,lhd->ehd", prob_half, attn_heads, preferred_element_type=jnp.float32
        ).astype(jnp.bfloat16)
        grad_normed = times_transposed(grad_query.reshape(dec_rows, inner_width), query_weight)
        scaled_grad = gain_row * grad_normed
        branch = inv_rms * scaled_grad - in_float * inv_rms * inv_rms * inv_rms * jnp.mean(
            in_float * scaled_grad, axis=1, keepdims=True
        )
        grad_input = (grad_y.astype(jnp.float32) + branch).astype(jnp.bfloat16)
        return (
            grad_input,
            grad_key.reshape(enc_rows, inner_width),
            grad_value.reshape(enc_rows, inner_width),
        )

    zero_input = jnp.zeros((dec_rows, width), jnp.bfloat16)
    zero_enc = jnp.zeros((enc_rows, inner_width), jnp.bfloat16)

    def loop_body(step_index, state_now):
        grad_now, grad_done, key_grad, value_grad = state_now
        is_active = my_section == section_count - 1 - step_index
        grad_done, key_grad, value_grad = lax.cond(
            is_active, lambda: backward_step(grad_now), lambda: (grad_done, key_grad, value_grad)
        )
        grad_now = from_behind(grad_done, "section", -1)
        return (grad_now, grad_done, key_grad, value_grad)

    grad_now, grad_done, key_grad, value_grad = lax.fori_loop(
        0, section_count - 1, loop_body, (grad_out[0], zero_input, zero_enc, zero_enc)
    )
    grad_done, key_grad, value_grad = lax.cond(
        my_section == 0, lambda: backward_step(grad_now), lambda: (grad_done, key_grad, value_grad)
    )
    enc_grad = lax.psum_scatter(
        (
            times_transposed(key_grad, key_weight) + times_transposed(value_grad, value_weight)
        ).astype(jnp.bfloat16),
        "section",
        scatter_dimension=0,
        tiled=True,
    )
    return (grad_done[None, None], enc_grad[None])

CORES = 2
ANY = pl.BlockSpec(memory_space=pl.ANY)
SMEM = pl.BlockSpec(memory_space=pltpu.SMEM)
VMEM = pl.BlockSpec(memory_space=pltpu.VMEM)
F32, BF16 = jnp.float32, jnp.bfloat16


def plan_fits(mesh_shape, dims):
    sections, ranks = mesh_shape["section"], mesh_shape["dp"]
    return sections == 4 and dims == ranks * sections * HEAD and ranks == 8


def dot_nt(a, b):
    return lax.dot_general(a, b, (((1,), (1,)), ((), ())), preferred_element_type=F32)


def dot_tn(a, b):
    return lax.dot_general(a, b, (((0,), (0,)), ((), ())), preferred_element_type=F32)


def dot_nn(a, b):
    return jnp.dot(a, b, preferred_element_type=F32)


def call(body, outs, inputs, specs, scratch, flops, size, out_specs=None, aliases=None):
    return list(pl.pallas_call(
        body,
        out_shape=outs,
        in_specs=specs,
        out_specs=[VMEM] * len(outs) if out_specs is None else out_specs,
        scratch_shapes=scratch,
        input_output_aliases=aliases or {},
        cost_estimate=pl.CostEstimate(flops=flops, bytes_accessed=size, transcendentals=0),
        compiler_params=pltpu.CompilerParams(vmem_limit_bytes=56 * 2**20),
    )(*inputs))


def choose(sources, index, target, sem):
    for i, source in enumerate(sources):

        @pl.when(index == i)
        def _(source=source):
            pltpu.make_async_copy(source, target, sem).start()

    return pltpu.make_async_copy(sources[0], target, sem)


def pieces_body(sections, me_ref, q_ref, k_ref, v_ref, o_ref, *rest):
    outs, buf, sems = rest[:sections], rest[sections], rest[sections + 1]
    me = me_ref[0]
    rows, inner = q_ref.shape
    part = inner // sections
    group = sections * HEAD
    lane = lax.broadcasted_iota(jnp.int32, (rows, 2 * HEAD), 1)
    waits = []
    for p in range(sections):
        for i, ref in enumerate((q_ref, k_ref, v_ref)):
            for m in range(part // (2 * HEAD)):
                at = 2 * group * m + 2 * HEAD * (p // 2)
                low, high = ref[:, at : at + 2 * HEAD], ref[:, at + group : at + group + 2 * HEAD]
                if p % 2 == 0:
                    high = jnp.concatenate([high[:, HEAD:], high[:, :HEAD]], axis=1)
                else:
                    low = jnp.concatenate([low[:, HEAD:], low[:, :HEAD]], axis=1)
                to = part * i + 2 * HEAD * m
                buf[p, :, to : to + 2 * HEAD] = jnp.where(lane < HEAD, low, high)
        for i in range(sections):
            buf[p, HEAD * i : HEAD * (i + 1), 3 * part :] = o_ref[
                HEAD * p : HEAD * (p + 1), part * i : part * (i + 1)
            ]
        for k in range(sections):

            @pl.when((me ^ k) == p)
            def _(k=k, p=p):
                pltpu.make_async_copy(buf.at[p], outs[k], sems.at[p]).start()

        waits.append(pltpu.make_async_copy(buf.at[p], outs[0], sems.at[p]))
    for w in waits:
        w.wait()


def forward_body(sections, section, table, candidates, me_ref, *refs):
    xs, packs, gs = refs[:sections], refs[sections : 2 * sections], refs[2 * sections :][:candidates]
    refs = refs[2 * sections + candidates :]
    q_out, k_out, v_out, prob_out, x_rows, inv_rows, gain_out, x_buf, enc, w_buf, sems = refs
    me = me_ref[0]
    x_copy = choose(xs, me ^ section, x_buf, sems.at[0])
    part = q_out.shape[1]
    which = lookup(table, me)
    w_copies = [
        choose(
            [g.at[:, part * i : part * (i + 1)] for g in gs], which, w_buf.at[i], sems.at[1 + i]
        )
        for i in range(3)
    ]
    rows = packs[0].shape[0] - 16
    gain = jnp.zeros((1, x_buf.shape[1]), F32)
    valid = jnp.zeros((1, sections * rows), F32)
    for k in range(sections):
        enc[pl.ds(pl.multiple_of((me ^ k) * rows, rows), rows), :] = packs[k][:rows, :]
        tail = packs[k][rows : rows + 16, :].astype(F32)
        valid = valid + tail[0:1, : sections * rows]
        gain = gain + jnp.where(k == (me ^ section), tail[1:2, :], 0.0)
    gain_out[...] = jnp.broadcast_to(gain, gain_out.shape)
    x_copy.wait()
    x = x_buf[...].astype(F32)
    inv = lax.rsqrt(jnp.mean(x * x, axis=1, keepdims=True) + 1e-06)
    block = x_rows.shape[0]
    start = pl.multiple_of(me * block, block)
    x_mine = x_buf[pl.ds(start, block), :]
    x_rows[...] = x_mine
    mine = x_mine.astype(F32)
    inv_rows[...] = jnp.broadcast_to(
        lax.rsqrt(jnp.mean(mine * mine, axis=1, keepdims=True) + 1e-06), inv_rows.shape
    )
    x_buf[...] = (x * inv * gain).astype(BF16)
    for i, (source, target) in enumerate(((x_buf, q_out), (enc, k_out), (enc, v_out))):
        w_copies[i].wait()
        target[...] = dot_nn(source[...], w_buf[i]).astype(BF16)
    lane = lax.broadcasted_iota(jnp.int32, (q_out.shape[0], 2 * HEAD), 1)
    for pair in range(part // (2 * HEAD)):
        cols = slice(2 * HEAD * pair, 2 * HEAD * (pair + 1))
        q, k = q_out[:, cols], k_out[:, cols]
        for h in range(2):
            scores = dot_nt(jnp.where((lane < HEAD) == (h == 0), q, 0), k)
            raw = jnp.exp(scores) * valid
            prob_out[2 * pair + h] = (raw / jnp.sum(raw, axis=1, keepdims=True)).astype(BF16)


def lookup(table, me):
    value = jnp.int32(table[0])
    for i in range(1, len(table)):
        value = jnp.where(me == i, jnp.int32(table[i]), value)
    return value


def chain_body(sections, table, candidates, whole, me_ref, *refs):
    count = 1 if whole else sections
    grads, refs = refs[:count], refs[count:]
    gs, refs = refs[:candidates], refs[candidates:]
    k_ref, v_ref, prob_ref = refs[:3]
    outs, refs = refs[3 : 3 + sections], refs[3 + sections :]
    score_out, attn_out, grad, gq, total, w_buf, sems = refs
    me = me_ref[0]
    part = k_ref.shape[1]
    which = lookup(table, me)
    o_copy, q_copy = [
        choose([g.at[:, part * i : part * (i + 1)] for g in gs], which, w_buf.at[j], sems.at[j])
        for j, i in ((0, 3), (1, 0))
    ]
    block = total.shape[0] // sections
    if whole:
        grad = grads[0]
    else:
        for k in range(sections):
            grad[pl.ds(pl.multiple_of((me ^ k) * block, block), block), :] = grads[k][...]
    o_copy.wait()
    ranks = part // HEAD
    attn = jnp.zeros((grad.shape[0], part), F32)
    for i in range(sections):
        weight = jnp.concatenate(
            [
                w_buf[0, (sections * r + i) * HEAD : (sections * r + i + 1) * HEAD, :]
                for r in range(ranks)
            ]
        )
        attn = attn + dot_nt(grad[:, part * i : part * (i + 1)], weight)
    attn_out[...] = attn.astype(BF16)
    lane = lax.broadcasted_iota(jnp.int32, (attn_out.shape[0], 2 * HEAD), 1)
    for pair in range(part // (2 * HEAD)):
        cols = slice(2 * HEAD * pair, 2 * HEAD * (pair + 1))
        a, v, k = attn_out[:, cols], v_ref[:, cols], k_ref[:, cols]
        got = []
        for h in range(2):
            grad_prob = dot_nt(jnp.where((lane < HEAD) == (h == 0), a, 0), v)
            prob = prob_ref[2 * pair + h].astype(F32)
            inner = jnp.sum(prob * grad_prob, axis=1, keepdims=True)
            score = (prob * (grad_prob - inner)).astype(BF16)
            score_out[2 * pair + h] = score
            got.append(dot_nn(score, k))
        gq[:, cols] = jnp.where(lane < HEAD, got[0], got[1]).astype(BF16)
    q_copy.wait()
    total[...] = dot_nt(gq[...], w_buf[1]).astype(BF16)
    for j in range(sections):
        outs[j][...] = total[pl.ds(pl.multiple_of((me ^ j) * block, block), block), :]


def encoder_body(sections, table, candidates, first, last, me_ref, *refs):
    gs, refs = refs[:candidates], refs[candidates:]
    score_ref, prob_ref, attn_ref, q_ref = refs[:4]
    refs = refs[4:]
    if not first:
        acc_in, refs = refs[0], refs[1:]
    if last:
        outs, refs = refs[:sections], refs[sections:]
    else:
        acc_out, refs = refs[0], refs[1:]
    gk, gv, total, w_buf, sems = refs
    me = me_ref[0]
    part = q_ref.shape[1]
    which = lookup(table, me)
    copies = [
        choose([g.at[:, part * i : part * (i + 1)] for g in gs], which, w_buf.at[i - 1], sems.at[i - 1])
        for i in (1, 2)
    ]
    lane = lax.broadcasted_iota(jnp.int32, (q_ref.shape[0], 2 * HEAD), 1)
    for pair in range(part // (2 * HEAD)):
        cols = slice(2 * HEAD * pair, 2 * HEAD * (pair + 1))
        a, q = attn_ref[:, cols], q_ref[:, cols]
        ks = [dot_tn(score_ref[2 * pair + h], q) for h in range(2)]
        vs = [dot_tn(prob_ref[2 * pair + h], a) for h in range(2)]
        gk[:, cols] = jnp.where(lane < HEAD, ks[0], ks[1]).astype(BF16)
        gv[:, cols] = jnp.where(lane < HEAD, vs[0], vs[1]).astype(BF16)
    for c in copies:
        c.wait()
    value = dot_nt(gk[...], w_buf[0]) + dot_nt(gv[...], w_buf[1])
    if not first:
        value = value + acc_in[...]
    if not last:
        acc_out[...] = value
    else:
        total[...] = value.astype(BF16)
        block = total.shape[0] // sections
        for j in range(sections):
            outs[j][...] = total[pl.ds(pl.multiple_of((me ^ j) * block, block), block), :]


def finish_body(count, me_ref, *refs):
    terms, refs = refs[:4], refs[4:]
    grads, refs = refs[:count], refs[count:]
    x_ref, inv_ref, gain_ref, out = refs
    total = terms[0][...].astype(F32)
    for t in terms[1:]:
        total = total + t[...].astype(F32)
    scaled = gain_ref[0:1, :] * total
    x, inv = x_ref[...].astype(F32), inv_ref[:, 0:1]
    branch = inv * scaled - x * inv * inv * inv * jnp.mean(x * scaled, axis=1, keepdims=True)
    block = out.shape[0]
    me = me_ref[0]
    if grads[0].shape[0] == block:
        grad = grads[0][...]
    else:
        grad = grads[0][pl.ds(pl.multiple_of(me * block, block), block), :]
    out[...] = (grad.astype(F32) + branch).astype(BF16)


def head_device(
    hidden_in, grad_out, encoder_out, enc_valid, norm_gain, w_query, w_key, w_value, w_out
):
    sections = lax.axis_size("section")
    ranks = lax.axis_size("dp")
    levels = ranks // CORES
    me = lax.axis_index("section")
    me_ref = jnp.reshape(me, (1,)).astype(jnp.int32)
    axes = ("section", "dp")
    shard, inner = w_query.shape[1], w_query.shape[2]
    width = hidden_in.shape[3]
    dec_rows = hidden_in.shape[2]
    enc_rows = encoder_out.shape[1]
    part = inner // sections
    heads = part // HEAD
    block = dec_rows // sections
    keys = enc_rows * sections

    def peer(array, k):
        pairs = [
            (s * ranks + r, (s ^ k) * ranks + r) for s in range(sections) for r in range(ranks)
        ]
        return lax.ppermute(array, axes, pairs)

    def peers(arrays):
        return [arrays[0]] + [peer(arrays[k], k) for k in range(1, sections)]

    def shape(dims, dtype=BF16):
        return jax.ShapeDtypeStruct(dims, dtype)

    pieces = call(
        functools.partial(pieces_body, sections),
        [shape((shard, inner))] * sections,
        [me_ref, w_query[0], w_key[0], w_value[0], w_out[0]],
        [SMEM] + [VMEM] * 4,
        [pltpu.VMEM((sections, shard, inner), BF16), pltpu.SemaphoreType.DMA((sections,))],
        0,
        8 * shard * inner * sections,
        out_specs=[ANY] * sections,
    )
    valid_row = lax.dynamic_update_slice(
        jnp.zeros((1, width), BF16), enc_valid.astype(BF16), (0, me * enc_rows)
    )
    pack = jnp.concatenate([encoder_out[0], valid_row, norm_gain, jnp.zeros((14, width), BF16)])
    packs = peers([pack] * sections)
    arrived = peers(pieces)
    hidden = peers([hidden_in[0, 0]] * sections)

    order = [[i] + [s for s in reversed(range(sections)) if s != i] for i in range(sections)]

    def gather(array):
        return lax.all_gather(array, "dp", axis=0, tiled=True)

    held = [gather(arrived[0])]
    for turn in range(1, sections):
        k = me ^ lookup([order[i][turn] for i in range(sections)], me)
        value = arrived[1]
        for j in range(2, sections):
            value = jnp.where(k == j, arrived[j], value)
        held.append(gather(value))

    gemm = 2 * dec_rows * width * part
    grads, whole = [grad_out[0]], True
    done, acc = [None] * sections, None
    rows_spec = shape((block, width))
    for s in reversed(range(sections)):
        turns = sorted({order[i].index(s) for i in range(sections)})
        table = [turns.index(order[i].index(s)) for i in range(sections)]
        weights = [held[t] for t in turns]
        n = len(weights)
        q, k, v, prob, x_rows, inv_rows, gain = call(
            functools.partial(forward_body, sections, s, table, n),
            [shape((dec_rows, part)), shape((keys, part)), shape((keys, part))]
            + [shape((heads, dec_rows, keys)), rows_spec]
            + [shape((block, 128), F32), shape((8, width), F32)],
            [me_ref] + hidden + packs + weights,
            [SMEM] + [ANY] * sections + [VMEM] * sections + [ANY] * n,
            [
                pltpu.VMEM((dec_rows, width), BF16),
                pltpu.VMEM((keys, width), BF16),
                pltpu.VMEM((3, width, part), BF16),
                pltpu.SemaphoreType.DMA((4,)),
            ],
            3 * gemm,
            12 * width * part,
        )
        outs = call(
            functools.partial(chain_body, sections, table, n, whole),
            [rows_spec] * sections + [shape((heads, dec_rows, keys)), shape((dec_rows, part))],
            [me_ref] + grads + weights + [k, v, prob],
            [SMEM] + [VMEM] * len(grads) + [ANY] * n + [VMEM] * 3,
            [
                pltpu.VMEM((dec_rows, width), BF16),
                pltpu.VMEM((dec_rows, part), BF16),
                pltpu.VMEM((dec_rows, width), BF16),
                pltpu.VMEM((2, width, part), BF16),
                pltpu.SemaphoreType.DMA((2,)),
            ],
            2 * gemm,
            8 * width * part,
        )
        terms, score, attn = peers(outs[:sections]), outs[sections], outs[sections + 1]
        mine = call(
            functools.partial(finish_body, 1),
            [rows_spec],
            [me_ref] + terms + [grads[0], x_rows, inv_rows, gain],
            [SMEM] + [VMEM] * 8,
            [],
            block * width * 10,
            block * width * 20,
        )[0]
        grads, whole = peers([mine] * sections), False
        done[s] = grads
        first, last = s == sections - 1, s == 0
        acc = call(
            functools.partial(encoder_body, sections, table, n, first, last),
            [shape((enc_rows, width))] * sections if last else [shape((keys, width), F32)],
            [me_ref] + weights + [score, prob, attn, q] + ([] if first else acc),
            [SMEM] + [ANY] * n + [VMEM] * (4 if first else 5),
            [
                pltpu.VMEM((keys, part), BF16),
                pltpu.VMEM((keys, part), BF16),
                pltpu.VMEM((keys, width), BF16),
                pltpu.VMEM((2, width, part), BF16),
                pltpu.SemaphoreType.DMA((2,)),
            ],
            2 * gemm,
            8 * width * part,
        )
    enc_terms = peers(acc)

    def sum_body(*refs):
        total = refs[0][...].astype(F32)
        for r in refs[1:-1]:
            total = total + r[...].astype(F32)
        refs[-1][...] = total.astype(BF16)

    enc_grad = call(
        sum_body,
        [shape((enc_rows, width))],
        enc_terms,
        [VMEM] * sections,
        [],
        enc_rows * width * 4,
        enc_rows * width * 10,
    )[0]

    def result_body(me_ref, *refs):
        out, sems = refs[-2], refs[-1]
        me = me_ref[0]
        for k in range(sections):
            at = pl.ds(pl.multiple_of((me ^ k) * block, block), block)
            choose([refs[sections * s + k] for s in range(sections)], me, out.at[at], sems.at[k])
        for k in range(sections):
            at = pl.ds(pl.multiple_of((me ^ k) * block, block), block)
            pltpu.make_async_copy(refs[k], out.at[at], sems.at[k]).wait()

    result = call(
        result_body,
        [shape((dec_rows, width))],
        [me_ref] + [g for s in range(sections) for g in done[s]],
        [SMEM] + [ANY] * (sections * sections),
        [pltpu.SemaphoreType.DMA((sections,))],
        0,
        dec_rows * width * 4,
    )[0]
    return (result[None, None], enc_grad[None])


def solution(mesh):
    in_specs = (
        P("section", "dp", None, None),
        P("dp", None, None),
        P("dp", "section", None),
        P("dp", "section"),
        P("section", None),
        P("section", "dp", None),
        P("section", "dp", None),
        P("section", "dp", None),
        P("section", "dp", None),
    )
    out_specs = (P("section", "dp", None, None), P("dp", "section", None))

    def run(*args):
        per_device = head_device if plan_fits(mesh.shape, args[5].shape[2]) else relay_device
        return jax.shard_map(
            per_device, mesh=mesh, in_specs=in_specs, out_specs=out_specs, check_vma=False
        )(*args)

    return run
```

```python
import functools

import jax
import jax.numpy as jnp
from jax import lax
from jax.experimental import pallas as pl
from jax.experimental.pallas import tpu as pltpu
from jax.sharding import PartitionSpec as P

HEAD = 64


def from_behind(array, axis, by):
    length = lax.axis_size(axis)
    pairs = [(i, i + by) for i in range(length) if 0 <= i + by < length]
    return lax.ppermute(array, axis, pairs)


def times_transposed(left_side, right_side):
    return lax.dot_general(
        left_side, right_side, (((1,), (1,)), ((), ())), preferred_element_type=jnp.float32
    )


def project_keys(encoded, key_weight, value_weight):
    keys_all = jnp.dot(encoded, key_weight, preferred_element_type=jnp.float32).astype(jnp.bfloat16)
    values_all = jnp.dot(encoded, value_weight, preferred_element_type=jnp.float32).astype(
        jnp.bfloat16
    )
    return (keys_all, values_all)


def relay_device(
    hidden_in, grad_out, encoder_out, enc_valid, norm_gain, w_query, w_key, w_value, w_out
):
    section_count = lax.axis_size("section")
    my_section = lax.axis_index("section")
    valid_half = enc_valid.astype(jnp.bfloat16)
    encoded_all, valid_all = (
        lax.all_gather(encoder_out, "section", axis=1, tiled=True),
        lax.all_gather(valid_half, "section", axis=1, tiled=True),
    )
    encoded = encoded_all[0]
    valid_keys = valid_all[0].astype(jnp.float32)
    query_full, key_full, value_full, out_full = (
        lax.all_gather(w_query, "dp", axis=1, tiled=True),
        lax.all_gather(w_key, "dp", axis=1, tiled=True),
        lax.all_gather(w_value, "dp", axis=1, tiled=True),
        lax.all_gather(w_out, "dp", axis=1, tiled=True),
    )
    keys_all, values_all = project_keys(encoded, key_full[0], value_full[0])
    query_weight = query_full[0]
    key_weight = key_full[0]
    value_weight = value_full[0]
    out_weight = out_full[0]
    dec_rows, width = (hidden_in.shape[2], hidden_in.shape[3])
    enc_rows = encoded.shape[0]
    inner_width = query_weight.shape[1]
    head_count = inner_width // HEAD
    in_float = hidden_in[0, 0].astype(jnp.float32)
    gain_row = norm_gain[0].astype(jnp.float32)
    inv_rms = lax.rsqrt(jnp.mean(in_float * in_float, axis=1, keepdims=True) + 1e-06)
    normed = (in_float * inv_rms * gain_row).astype(jnp.bfloat16)
    queries = jnp.dot(normed, query_weight, preferred_element_type=jnp.float32).astype(jnp.bfloat16)
    query_heads = queries.reshape(dec_rows, head_count, HEAD)
    key_heads = keys_all.reshape(enc_rows, head_count, HEAD)
    value_heads = values_all.reshape(enc_rows, head_count, HEAD)
    scores = jnp.einsum("lhd,ehd->hle", query_heads, key_heads, preferred_element_type=jnp.float32)
    raw = jnp.exp(scores) * valid_keys[None, None, :]
    attn_prob = raw / jnp.sum(raw, axis=2, keepdims=True)
    prob_half = attn_prob.astype(jnp.bfloat16)

    def backward_step(grad_y):
        grad_attn = times_transposed(grad_y, out_weight).astype(jnp.bfloat16)
        attn_heads = grad_attn.reshape(dec_rows, head_count, HEAD)
        grad_prob = jnp.einsum(
            "lhd,ehd->hle", attn_heads, value_heads, preferred_element_type=jnp.float32
        )
        inner_sum = jnp.sum(attn_prob * grad_prob, axis=2, keepdims=True)
        grad_scores = (attn_prob * (grad_prob - inner_sum)).astype(jnp.bfloat16)
        grad_query = jnp.einsum(
            "hle,ehd->lhd", grad_scores, key_heads, preferred_element_type=jnp.float32
        ).astype(jnp.bfloat16)
        grad_key = jnp.einsum(
            "hle,lhd->ehd", grad_scores, query_heads, preferred_element_type=jnp.float32
        ).astype(jnp.bfloat16)
        grad_value = jnp.einsum(
            "hle,lhd->ehd", prob_half, attn_heads, preferred_element_type=jnp.float32
        ).astype(jnp.bfloat16)
        grad_normed = times_transposed(grad_query.reshape(dec_rows, inner_width), query_weight)
        scaled_grad = gain_row * grad_normed
        branch = inv_rms * scaled_grad - in_float * inv_rms * inv_rms * inv_rms * jnp.mean(
            in_float * scaled_grad, axis=1, keepdims=True
        )
        grad_input = (grad_y.astype(jnp.float32) + branch).astype(jnp.bfloat16)
        return (
            grad_input,
            grad_key.reshape(enc_rows, inner_width),
            grad_value.reshape(enc_rows, inner_width),
        )

    zero_input = jnp.zeros((dec_rows, width), jnp.bfloat16)
    zero_enc = jnp.zeros((enc_rows, inner_width), jnp.bfloat16)

    def loop_body(step_index, state_now):
        grad_now, grad_done, key_grad, value_grad = state_now
        is_active = my_section == section_count - 1 - step_index
        grad_done, key_grad, value_grad = lax.cond(
            is_active, lambda: backward_step(grad_now), lambda: (grad_done, key_grad, value_grad)
        )
        grad_now = from_behind(grad_done, "section", -1)
        return (grad_now, grad_done, key_grad, value_grad)

    grad_now, grad_done, key_grad, value_grad = lax.fori_loop(
        0, section_count - 1, loop_body, (grad_out[0], zero_input, zero_enc, zero_enc)
    )
    grad_done, key_grad, value_grad = lax.cond(
        my_section == 0, lambda: backward_step(grad_now), lambda: (grad_done, key_grad, value_grad)
    )
    enc_grad = lax.psum_scatter(
        (
            times_transposed(key_grad, key_weight) + times_transposed(value_grad, value_weight)
        ).astype(jnp.bfloat16),
        "section",
        scatter_dimension=0,
        tiled=True,
    )
    return (grad_done[None, None], enc_grad[None])

CORES = 2
ANY = pl.BlockSpec(memory_space=pl.ANY)
SMEM = pl.BlockSpec(memory_space=pltpu.SMEM)
VMEM = pl.BlockSpec(memory_space=pltpu.VMEM)
F32, BF16 = jnp.float32, jnp.bfloat16


def plan_fits(mesh_shape, dims):
    sections, ranks = mesh_shape["section"], mesh_shape["dp"]
    return sections == 4 and dims == ranks * sections * HEAD and ranks == 8


def dot_nt(a, b):
    return lax.dot_general(a, b, (((1,), (1,)), ((), ())), preferred_element_type=F32)


def dot_tn(a, b):
    return lax.dot_general(a, b, (((0,), (0,)), ((), ())), preferred_element_type=F32)


def dot_nn(a, b):
    return jnp.dot(a, b, preferred_element_type=F32)


def call(body, outs, inputs, specs, scratch, flops, size, out_specs=None, after=()):
    count = len(inputs)

    def kernel(*refs):
        body(*refs[:count], *refs[count + len(after) :])

    return list(pl.pallas_call(
        kernel,
        out_shape=outs,
        in_specs=specs + [ANY] * len(after),
        out_specs=[VMEM] * len(outs) if out_specs is None else out_specs,
        scratch_shapes=scratch,
        cost_estimate=pl.CostEstimate(flops=flops, bytes_accessed=size, transcendentals=0),
        compiler_params=pltpu.CompilerParams(vmem_limit_bytes=56 * 2**20),
    )(*inputs, *after))


def choose(sources, index, target, sem):
    if len(sources) == 1:
        copy = pltpu.make_async_copy(sources[0], target, sem)
        copy.start()
        return copy
    for i, source in enumerate(sources):

        @pl.when(index == i)
        def _(source=source):
            pltpu.make_async_copy(source, target, sem).start()

    return pltpu.make_async_copy(sources[0], target, sem)


def pieces_body(sections, me_ref, q_ref, k_ref, v_ref, o_ref, *rest):
    outs, buf, sems = rest[: 2 * sections], rest[2 * sections], rest[2 * sections + 1]
    me = me_ref[0]
    rows, inner = q_ref.shape
    part = inner // sections
    group = sections * HEAD
    lane = lax.broadcasted_iota(jnp.int32, (rows, 2 * HEAD), 1)
    waits = []
    for p in range(sections):
        for i, ref in enumerate((q_ref, k_ref, v_ref)):
            for m in range(part // (2 * HEAD)):
                at = 2 * group * m + 2 * HEAD * (p // 2)
                low, high = ref[:, at : at + 2 * HEAD], ref[:, at + group : at + group + 2 * HEAD]
                if p % 2 == 0:
                    high = jnp.concatenate([high[:, HEAD:], high[:, :HEAD]], axis=1)
                else:
                    low = jnp.concatenate([low[:, HEAD:], low[:, :HEAD]], axis=1)
                to = part * i + 2 * HEAD * m
                buf[p, :, to : to + 2 * HEAD] = jnp.where(lane < HEAD, low, high)
        for i in range(sections):
            buf[p, HEAD * i : HEAD * (i + 1), 3 * part :] = o_ref[
                HEAD * p : HEAD * (p + 1), part * i : part * (i + 1)
            ]
        for half in range(2):
            cut = buf.at[p, :, pl.ds(half * 2 * part, 2 * part)]
            for k in range(sections):

                @pl.when((me ^ k) == p)
                def _(k=k, p=p, cut=cut, half=half):
                    to = outs[sections * half + k]
                    pltpu.make_async_copy(cut, to, sems.at[2 * p + half]).start()

            waits.append(pltpu.make_async_copy(cut, outs[0], sems.at[2 * p + half]))
    for w in waits:
        w.wait()


def pick_body(tables, me_ref, *refs):
    sources, target, sems = refs[:-2], refs[-2], refs[-1]
    width = sources[0].shape[1]
    copies = [
        choose(sources, lookup(table, me_ref[0]), target.at[:, width * i : width * (i + 1)], sems.at[i])
        for i, table in enumerate(tables)
    ]
    for copy in copies:
        copy.wait()


def encoder_rows_body(sections, me_ref, *refs):
    packs, (enc, valid_out, gain_out) = refs[:sections], refs[sections:]
    me = me_ref[0]
    rows = enc.shape[0] // sections
    valid = jnp.zeros((1, enc.shape[0]), F32)
    for k in range(sections):
        enc[pl.ds(pl.multiple_of((me ^ k) * rows, rows), rows), :] = packs[k][:rows, :]
        tail = packs[k][rows : rows + 16, :].astype(F32)
        valid = valid + tail[0:1, : enc.shape[0]]
        gain_out[me ^ k] = jnp.broadcast_to(tail[1:2, :], gain_out.shape[1:])
    valid_out[...] = jnp.broadcast_to(valid, valid_out.shape)


def forward_body(sections, section, source, me_ref, *refs):
    xs, refs = refs[:sections], refs[sections:]
    enc, valid_ref, gain_ref, refs = refs[0], refs[1], refs[2], refs[3:]
    gs, refs = refs[: source.count], refs[source.count :]
    q_out, k_out, prob_out, x_rows, inv_rows, x_buf, w_buf, sems = refs
    me = me_ref[0]
    x_copy = choose(xs, me ^ section, x_buf, sems.at[0])
    part = q_out.shape[1]
    w_copies = [source.load(gs, me, i, part, w_buf.at[i], sems.at[1 + i]) for i in range(2)]
    gain, valid = gain_ref[section, 0:1, :], valid_ref[0:1, :]
    w_copies[1].wait()
    k_out[...] = dot_nn(enc[...], w_buf[1]).astype(BF16)
    x_copy.wait()
    x = x_buf[...].astype(F32)
    inv = lax.rsqrt(jnp.mean(x * x, axis=1, keepdims=True) + 1e-06)
    block = x_rows.shape[0]
    x_mine = x_buf[pl.ds(pl.multiple_of(me * block, block), block), :]
    x_rows[...] = x_mine
    mine = x_mine.astype(F32)
    inv_rows[...] = jnp.broadcast_to(
        lax.rsqrt(jnp.mean(mine * mine, axis=1, keepdims=True) + 1e-06), inv_rows.shape
    )
    x_buf[...] = (x * inv * gain).astype(BF16)
    w_copies[0].wait()
    q_out[...] = dot_nn(x_buf[...], w_buf[0]).astype(BF16)
    lane = lax.broadcasted_iota(jnp.int32, (q_out.shape[0], 2 * HEAD), 1)
    for pair in range(part // (2 * HEAD)):
        cols = slice(2 * HEAD * pair, 2 * HEAD * (pair + 1))
        q, k = q_out[:, cols], k_out[:, cols]
        for h in range(2):
            scores = dot_nt(jnp.where((lane < HEAD) == (h == 0), q, 0), k)
            raw = jnp.exp(scores) * valid
            prob_out[2 * pair + h] = (raw / jnp.sum(raw, axis=1, keepdims=True)).astype(BF16)


class Source:
    def __init__(self, arrays, places, table):
        self.arrays, self.places, self.table = arrays, places, table
        self.count = len(arrays)

    def load(self, refs, me, i, part, target, sem):
        views = [refs[a].at[:, part * (2 * h + i) : part * (2 * h + i + 1)] for a, h in self.places]
        return choose(views, lookup(self.table, me), target, sem)


def lookup(table, me):
    value = jnp.int32(table[0])
    for i in range(1, len(table)):
        value = jnp.where(me == i, jnp.int32(table[i]), value)
    return value


def chain_body(sections, first, second, whole, me_ref, *refs):
    grads, refs = (refs[:1], refs[1:]) if whole else (refs[:sections], refs[sections:])
    g1, refs = refs[: first.count], refs[first.count :]
    g2, refs = refs[: second.count], refs[second.count :]
    k_ref, enc, prob_ref = refs[:3]
    outs, refs = refs[3 : 3 + sections], refs[3 + sections :]
    score_out, attn_out, grad, v_ref, gq, total, w_buf, sems = refs
    me = me_ref[0]
    part = k_ref.shape[1]
    v_copy = second.load(g2, me, 0, part, w_buf.at[2], sems.at[2])
    o_copy = second.load(g2, me, 1, part, w_buf.at[0], sems.at[0])
    q_copy = first.load(g1, me, 0, part, w_buf.at[1], sems.at[1])
    block = total.shape[0] // sections
    if whole:
        grad = grads[0]
    else:
        for k in range(sections):
            grad[pl.ds(pl.multiple_of((me ^ k) * block, block), block), :] = grads[k][...]
    v_copy.wait()
    v_ref[...] = dot_nn(enc[...], w_buf[2]).astype(BF16)
    o_copy.wait()
    ranks = part // HEAD
    attn = jnp.zeros((grad.shape[0], part), F32)
    for i in range(sections):
        weight = jnp.concatenate(
            [
                w_buf[0, (sections * r + i) * HEAD : (sections * r + i + 1) * HEAD, :]
                for r in range(ranks)
            ]
        )
        attn = attn + dot_nt(grad[:, part * i : part * (i + 1)], weight)
    attn_out[...] = attn.astype(BF16)
    lane = lax.broadcasted_iota(jnp.int32, (attn_out.shape[0], 2 * HEAD), 1)
    for pair in range(part // (2 * HEAD)):
        cols = slice(2 * HEAD * pair, 2 * HEAD * (pair + 1))
        a, v, k = attn_out[:, cols], v_ref[:, cols], k_ref[:, cols]
        got = []
        for h in range(2):
            grad_prob = dot_nt(jnp.where((lane < HEAD) == (h == 0), a, 0), v)
            prob = prob_ref[2 * pair + h].astype(F32)
            inner = jnp.sum(prob * grad_prob, axis=1, keepdims=True)
            score = (prob * (grad_prob - inner)).astype(BF16)
            score_out[2 * pair + h] = score
            got.append(dot_nn(score, k))
        gq[:, cols] = jnp.where(lane < HEAD, got[0], got[1]).astype(BF16)
    q_copy.wait()
    total[...] = dot_nt(gq[...], w_buf[1]).astype(BF16)
    for j in range(sections):
        outs[j][...] = total[pl.ds(pl.multiple_of((me ^ j) * block, block), block), :]


def encoder_body(sections, one, two, first, last, me_ref, *refs):
    g1, refs = refs[: one.count], refs[one.count :]
    g2, refs = refs[: two.count], refs[two.count :]
    score_ref, prob_ref, attn_ref, q_ref = refs[:4]
    refs = refs[4:]
    if not first:
        acc_in, refs = refs[0], refs[1:]
    if last:
        outs, refs = refs[:sections], refs[sections:]
    else:
        acc_out, refs = refs[0], refs[1:]
    gk, gv, total, w_buf, sems = refs
    me = me_ref[0]
    part = q_ref.shape[1]
    copies = [
        one.load(g1, me, 1, part, w_buf.at[0], sems.at[0]),
        two.load(g2, me, 0, part, w_buf.at[1], sems.at[1]),
    ]
    lane = lax.broadcasted_iota(jnp.int32, (q_ref.shape[0], 2 * HEAD), 1)
    for pair in range(part // (2 * HEAD)):
        cols = slice(2 * HEAD * pair, 2 * HEAD * (pair + 1))
        a, q = attn_ref[:, cols], q_ref[:, cols]
        ks = [dot_tn(score_ref[2 * pair + h], q) for h in range(2)]
        vs = [dot_tn(prob_ref[2 * pair + h], a) for h in range(2)]
        gk[:, cols] = jnp.where(lane < HEAD, ks[0], ks[1]).astype(BF16)
        gv[:, cols] = jnp.where(lane < HEAD, vs[0], vs[1]).astype(BF16)
    for c in copies:
        c.wait()
    value = dot_nt(gk[...], w_buf[0]) + dot_nt(gv[...], w_buf[1])
    if not first:
        value = value + acc_in[...]
    if not last:
        acc_out[...] = value
    else:
        total[...] = value.astype(BF16)
        block = total.shape[0] // sections
        for j in range(sections):
            outs[j][...] = total[pl.ds(pl.multiple_of((me ^ j) * block, block), block), :]


def finish_body(count, section, me_ref, *refs):
    terms, refs = refs[:4], refs[4:]
    grads, refs = refs[:count], refs[count:]
    x_ref, inv_ref, gain_ref, out = refs
    total = terms[0][...].astype(F32)
    for t in terms[1:]:
        total = total + t[...].astype(F32)
    scaled = gain_ref[section, 0:1, :] * total
    x, inv = x_ref[...].astype(F32), inv_ref[:, 0:1]
    branch = inv * scaled - x * inv * inv * inv * jnp.mean(x * scaled, axis=1, keepdims=True)
    block = out.shape[0]
    me = me_ref[0]
    if grads[0].shape[0] == block:
        grad = grads[0][...]
    else:
        grad = grads[0][pl.ds(pl.multiple_of(me * block, block), block), :]
    out[...] = (grad.astype(F32) + branch).astype(BF16)


def head_device(
    hidden_in, grad_out, encoder_out, enc_valid, norm_gain, w_query, w_key, w_value, w_out
):
    sections = lax.axis_size("section")
    ranks = lax.axis_size("dp")
    levels = ranks // CORES
    me = lax.axis_index("section")
    me_ref = jnp.reshape(me, (1,)).astype(jnp.int32)
    axes = ("section", "dp")
    shard, inner = w_query.shape[1], w_query.shape[2]
    width = hidden_in.shape[3]
    dec_rows = hidden_in.shape[2]
    enc_rows = encoder_out.shape[1]
    part = inner // sections
    heads = part // HEAD
    block = dec_rows // sections
    keys = enc_rows * sections

    def peer(array, k):
        pairs = [
            (s * ranks + r, (s ^ k) * ranks + r) for s in range(sections) for r in range(ranks)
        ]
        return lax.ppermute(array, axes, pairs)

    def peers(arrays):
        return [arrays[0]] + [peer(arrays[k], k) for k in range(1, sections)]

    def shape(dims, dtype=BF16):
        return jax.ShapeDtypeStruct(dims, dtype)

    pieces = call(
        functools.partial(pieces_body, sections),
        [shape((shard, 2 * part))] * (2 * sections),
        [me_ref, w_query[0], w_key[0], w_value[0], w_out[0]],
        [SMEM] + [VMEM] * 4,
        [pltpu.VMEM((sections, shard, inner), BF16), pltpu.SemaphoreType.DMA((2 * sections,))],
        0,
        8 * shard * inner * sections,
        out_specs=[ANY] * (2 * sections),
    )
    valid_row = lax.dynamic_update_slice(
        jnp.zeros((1, width), BF16), enc_valid.astype(BF16), (0, me * enc_rows)
    )
    pack = jnp.concatenate([encoder_out[0], valid_row, norm_gain, jnp.zeros((14, width), BF16)])
    arrived = [peers(pieces[:sections]), peers(pieces[sections:])]
    packs = peers([pack] * sections)
    hidden = peers([hidden_in[0, 0]] * sections)
    encoded, valid, gains = call(
        functools.partial(encoder_rows_body, sections),
        [shape((keys, width)), shape((8, keys), F32), shape((sections, 8, width), F32)],
        [me_ref] + packs,
        [SMEM] + [VMEM] * sections,
        [],
        0,
        4 * keys * width,
    )

    order = [
        [(i, 0)]
        + [(s, h) for s in reversed(range(sections)) for h in range(2) if (s, h) != (i, 0)]
        for i in range(sections)
    ]
    spans = [(0, 1)] + [(t, t + 2) for t in range(1, 2 * sections - 1, 2)]
    spans += [(2 * sections - 1, 2 * sections)]
    held = []
    for low, high in spans:
        wanted = [
            [(i ^ order[i][turn][0], order[i][turn][1]) for i in range(sections)]
            for turn in range(low, high)
        ]
        unique = sorted(set(sum(wanted, [])))
        options = [arrived[h][k] for k, h in unique]
        if len(options) > 1:
            tables = [[unique.index(w) for w in want] for want in wanted]
            value = call(
                functools.partial(pick_body, tables),
                [shape((shard, options[0].shape[1] * (high - low)))],
                [me_ref] + options,
                [SMEM] + [ANY] * len(options),
                [pltpu.SemaphoreType.DMA((high - low,))],
                0,
                4 * options[0].size * (high - low),
            )[0]
        else:
            value = options[0]
        held.append(lax.all_gather(value, "dp", axis=0, tiled=True))
    place = {t: (j, t - low) for j, (low, high) in enumerate(spans) for t in range(low, high)}

    def source(s, h):
        found = [place[order[i].index((s, h))] for i in range(sections)]
        places = sorted(set(found))
        arrays = sorted({j for j, _ in places})
        return Source(
            [held[j] for j in arrays],
            [(arrays.index(j), at) for j, at in places],
            [places.index(f) for f in found],
        )

    gemm = 2 * dec_rows * width * part
    rows_spec = shape((block, width))
    halves = [(source(s, 0), source(s, 1)) for s in range(sections)]

    def forward(s, after):
        one = halves[s][0]
        return call(
            functools.partial(forward_body, sections, s, one),
            [shape((dec_rows, part)), shape((keys, part))]
            + [shape((heads, dec_rows, keys)), rows_spec, shape((block, 128), F32)],
            [me_ref] + hidden + [encoded, valid, gains] + one.arrays,
            [SMEM] + [ANY] * sections + [VMEM] * 3 + [ANY] * one.count,
            [
                pltpu.VMEM((dec_rows, width), BF16),
                pltpu.VMEM((2, width, part), BF16),
                pltpu.SemaphoreType.DMA((3,)),
            ],
            2 * gemm,
            8 * width * part,
            after=after,
        )

    def chain(s, grads, k, prob, after):
        one, two = halves[s]
        return call(
            functools.partial(chain_body, sections, one, two, len(grads) == 1),
            [rows_spec] * sections + [shape((heads, dec_rows, keys)), shape((dec_rows, part))],
            [me_ref] + grads + one.arrays + two.arrays + [k, encoded, prob],
            [SMEM] + [VMEM] * len(grads) + [ANY] * (one.count + two.count) + [VMEM] * 3,
            [
                pltpu.VMEM((dec_rows, width), BF16),
                pltpu.VMEM((keys, part), BF16),
                pltpu.VMEM((dec_rows, part), BF16),
                pltpu.VMEM((dec_rows, width), BF16),
                pltpu.VMEM((3, width, part), BF16),
                pltpu.SemaphoreType.DMA((3,)),
            ],
            3 * gemm,
            12 * width * part,
            after=after,
        )

    def encoder(s, score, prob, attn, q, acc, after):
        one, two = halves[s]
        return call(
            functools.partial(encoder_body, sections, one, two, not acc, s == 0),
            [shape((enc_rows, width))] * sections if s == 0 else [shape((keys, width), F32)],
            [me_ref] + one.arrays + two.arrays + [score, prob, attn, q] + acc,
            [SMEM] + [ANY] * (one.count + two.count) + [VMEM] * (4 + len(acc)),
            [
                pltpu.VMEM((keys, part), BF16),
                pltpu.VMEM((keys, part), BF16),
                pltpu.VMEM((keys, width), BF16),
                pltpu.VMEM((2, width, part), BF16),
                pltpu.SemaphoreType.DMA((2,)),
            ],
            2 * gemm,
            8 * width * part,
            after=after,
        )

    grads = [grad_out[0]]
    done, acc, state = [None] * sections, [], None
    for s in reversed(range(sections)):
        q, k, prob, x_rows, inv_rows = forward(s, acc)
        outs = chain(s, grads, k, prob, acc)
        terms, score, attn = peers(outs[:sections]), outs[sections], outs[sections + 1]
        early = []
        if s == 0:
            acc = encoder(s, score, prob, attn, q, acc, [])
            early = [acc[0]]
        mine = call(
            functools.partial(finish_body, 1, s),
            [rows_spec],
            [me_ref] + terms + [grads[0], x_rows, inv_rows, gains],
            [SMEM] + [VMEM] * 8,
            [],
            block * width * 10,
            block * width * 20,
            after=early,
        )[0]
        grads = peers([mine] * sections)
        done[s] = grads
        if s > 0:
            acc = encoder(s, score, prob, attn, q, acc, [mine])
    enc_terms = peers(acc)

    def sum_body(*refs):
        total = refs[0][...].astype(F32)
        for r in refs[1:-1]:
            total = total + r[...].astype(F32)
        refs[-1][...] = total.astype(BF16)

    enc_grad = call(
        sum_body,
        [shape((enc_rows, width))],
        enc_terms,
        [VMEM] * sections,
        [],
        enc_rows * width * 4,
        enc_rows * width * 10,
    )[0]

    def result_body(me_ref, *refs):
        out, sems = refs[-2], refs[-1]
        me = me_ref[0]
        for k in range(sections):
            at = pl.ds(pl.multiple_of((me ^ k) * block, block), block)
            choose([refs[sections * s + k] for s in range(sections)], me, out.at[at], sems.at[k])
        for k in range(sections):
            at = pl.ds(pl.multiple_of((me ^ k) * block, block), block)
            pltpu.make_async_copy(refs[k], out.at[at], sems.at[k]).wait()

    result = call(
        result_body,
        [shape((dec_rows, width))],
        [me_ref] + [g for s in range(sections) for g in done[s]],
        [SMEM] + [ANY] * (sections * sections),
        [pltpu.SemaphoreType.DMA((sections,))],
        0,
        dec_rows * width * 4,
    )[0]
    return (result[None, None], enc_grad[None])


def solution(mesh):
    in_specs = (
        P("section", "dp", None, None),
        P("dp", None, None),
        P("dp", "section", None),
        P("dp", "section"),
        P("section", None),
        P("section", "dp", None),
        P("section", "dp", None),
        P("section", "dp", None),
        P("section", "dp", None),
    )
    out_specs = (P("section", "dp", None, None), P("dp", "section", None))

    def run(*args):
        per_device = head_device if plan_fits(mesh.shape, args[5].shape[2]) else relay_device
        return jax.shard_map(
            per_device, mesh=mesh, in_specs=in_specs, out_specs=out_specs, check_vma=False
        )(*args)

    return run
```

```python
import functools

import jax
import jax.numpy as jnp
from jax import lax
from jax.experimental import pallas as pl
from jax.experimental.pallas import tpu as pltpu
from jax.sharding import PartitionSpec as P

HEAD = 64


def from_behind(array, axis, by):
    length = lax.axis_size(axis)
    pairs = [(i, i + by) for i in range(length) if 0 <= i + by < length]
    return lax.ppermute(array, axis, pairs)


def times_transposed(left_side, right_side):
    return lax.dot_general(
        left_side, right_side, (((1,), (1,)), ((), ())), preferred_element_type=jnp.float32
    )


def project_keys(encoded, key_weight, value_weight):
    keys_all = jnp.dot(encoded, key_weight, preferred_element_type=jnp.float32).astype(jnp.bfloat16)
    values_all = jnp.dot(encoded, value_weight, preferred_element_type=jnp.float32).astype(
        jnp.bfloat16
    )
    return (keys_all, values_all)


def relay_device(
    hidden_in, grad_out, encoder_out, enc_valid, norm_gain, w_query, w_key, w_value, w_out
):
    section_count = lax.axis_size("section")
    my_section = lax.axis_index("section")
    valid_half = enc_valid.astype(jnp.bfloat16)
    encoded_all, valid_all = (
        lax.all_gather(encoder_out, "section", axis=1, tiled=True),
        lax.all_gather(valid_half, "section", axis=1, tiled=True),
    )
    encoded = encoded_all[0]
    valid_keys = valid_all[0].astype(jnp.float32)
    query_full, key_full, value_full, out_full = (
        lax.all_gather(w_query, "dp", axis=1, tiled=True),
        lax.all_gather(w_key, "dp", axis=1, tiled=True),
        lax.all_gather(w_value, "dp", axis=1, tiled=True),
        lax.all_gather(w_out, "dp", axis=1, tiled=True),
    )
    keys_all, values_all = project_keys(encoded, key_full[0], value_full[0])
    query_weight = query_full[0]
    key_weight = key_full[0]
    value_weight = value_full[0]
    out_weight = out_full[0]
    dec_rows, width = (hidden_in.shape[2], hidden_in.shape[3])
    enc_rows = encoded.shape[0]
    inner_width = query_weight.shape[1]
    head_count = inner_width // HEAD
    in_float = hidden_in[0, 0].astype(jnp.float32)
    gain_row = norm_gain[0].astype(jnp.float32)
    inv_rms = lax.rsqrt(jnp.mean(in_float * in_float, axis=1, keepdims=True) + 1e-06)
    normed = (in_float * inv_rms * gain_row).astype(jnp.bfloat16)
    queries = jnp.dot(normed, query_weight, preferred_element_type=jnp.float32).astype(jnp.bfloat16)
    query_heads = queries.reshape(dec_rows, head_count, HEAD)
    key_heads = keys_all.reshape(enc_rows, head_count, HEAD)
    value_heads = values_all.reshape(enc_rows, head_count, HEAD)
    scores = jnp.einsum("lhd,ehd->hle", query_heads, key_heads, preferred_element_type=jnp.float32)
    raw = jnp.exp(scores) * valid_keys[None, None, :]
    attn_prob = raw / jnp.sum(raw, axis=2, keepdims=True)
    prob_half = attn_prob.astype(jnp.bfloat16)

    def backward_step(grad_y):
        grad_attn = times_transposed(grad_y, out_weight).astype(jnp.bfloat16)
        attn_heads = grad_attn.reshape(dec_rows, head_count, HEAD)
        grad_prob = jnp.einsum(
            "lhd,ehd->hle", attn_heads, value_heads, preferred_element_type=jnp.float32
        )
        inner_sum = jnp.sum(attn_prob * grad_prob, axis=2, keepdims=True)
        grad_scores = (attn_prob * (grad_prob - inner_sum)).astype(jnp.bfloat16)
        grad_query = jnp.einsum(
            "hle,ehd->lhd", grad_scores, key_heads, preferred_element_type=jnp.float32
        ).astype(jnp.bfloat16)
        grad_key = jnp.einsum(
            "hle,lhd->ehd", grad_scores, query_heads, preferred_element_type=jnp.float32
        ).astype(jnp.bfloat16)
        grad_value = jnp.einsum(
            "hle,lhd->ehd", prob_half, attn_heads, preferred_element_type=jnp.float32
        ).astype(jnp.bfloat16)
        grad_normed = times_transposed(grad_query.reshape(dec_rows, inner_width), query_weight)
        scaled_grad = gain_row * grad_normed
        branch = inv_rms * scaled_grad - in_float * inv_rms * inv_rms * inv_rms * jnp.mean(
            in_float * scaled_grad, axis=1, keepdims=True
        )
        grad_input = (grad_y.astype(jnp.float32) + branch).astype(jnp.bfloat16)
        return (
            grad_input,
            grad_key.reshape(enc_rows, inner_width),
            grad_value.reshape(enc_rows, inner_width),
        )

    zero_input = jnp.zeros((dec_rows, width), jnp.bfloat16)
    zero_enc = jnp.zeros((enc_rows, inner_width), jnp.bfloat16)

    def loop_body(step_index, state_now):
        grad_now, grad_done, key_grad, value_grad = state_now
        is_active = my_section == section_count - 1 - step_index
        grad_done, key_grad, value_grad = lax.cond(
            is_active, lambda: backward_step(grad_now), lambda: (grad_done, key_grad, value_grad)
        )
        grad_now = from_behind(grad_done, "section", -1)
        return (grad_now, grad_done, key_grad, value_grad)

    grad_now, grad_done, key_grad, value_grad = lax.fori_loop(
        0, section_count - 1, loop_body, (grad_out[0], zero_input, zero_enc, zero_enc)
    )
    grad_done, key_grad, value_grad = lax.cond(
        my_section == 0, lambda: backward_step(grad_now), lambda: (grad_done, key_grad, value_grad)
    )
    enc_grad = lax.psum_scatter(
        (
            times_transposed(key_grad, key_weight) + times_transposed(value_grad, value_weight)
        ).astype(jnp.bfloat16),
        "section",
        scatter_dimension=0,
        tiled=True,
    )
    return (grad_done[None, None], enc_grad[None])

CORES = 2
ANY = pl.BlockSpec(memory_space=pl.ANY)
SMEM = pl.BlockSpec(memory_space=pltpu.SMEM)
VMEM = pl.BlockSpec(memory_space=pltpu.VMEM)
F32, BF16 = jnp.float32, jnp.bfloat16


def plan_fits(mesh_shape, dims):
    sections, ranks = mesh_shape["section"], mesh_shape["dp"]
    return sections == 4 and dims == ranks * sections * HEAD and ranks == 8


def dot_nt(a, b):
    return lax.dot_general(a, b, (((1,), (1,)), ((), ())), preferred_element_type=F32)


def dot_tn(a, b):
    return lax.dot_general(a, b, (((0,), (0,)), ((), ())), preferred_element_type=F32)


def dot_nn(a, b):
    return jnp.dot(a, b, preferred_element_type=F32)


def call(body, outs, inputs, specs, scratch, flops, size, out_specs=None, after=()):
    count = len(inputs)

    def kernel(*refs):
        body(*refs[:count], *refs[count + len(after) :])

    return list(pl.pallas_call(
        kernel,
        out_shape=outs,
        in_specs=specs + [ANY] * len(after),
        out_specs=[VMEM] * len(outs) if out_specs is None else out_specs,
        scratch_shapes=scratch,
        cost_estimate=pl.CostEstimate(flops=flops, bytes_accessed=size, transcendentals=0),
        compiler_params=pltpu.CompilerParams(vmem_limit_bytes=56 * 2**20),
    )(*inputs, *after))


def choose(sources, index, target, sem):
    if len(sources) == 1:
        copy = pltpu.make_async_copy(sources[0], target, sem)
        copy.start()
        return copy
    for i, source in enumerate(sources):

        @pl.when(index == i)
        def _(source=source):
            pltpu.make_async_copy(source, target, sem).start()

    return pltpu.make_async_copy(sources[0], target, sem)


def pieces_body(sections, me_ref, q_ref, k_ref, v_ref, o_ref, *rest):
    outs, buf, sems = rest[: 2 * sections], rest[2 * sections], rest[2 * sections + 1]
    me = me_ref[0]
    rows, inner = q_ref.shape
    part = inner // sections
    group = sections * HEAD
    lane = lax.broadcasted_iota(jnp.int32, (rows, 2 * HEAD), 1)
    waits = []
    for p in range(sections):
        for i, ref in enumerate((q_ref, k_ref, v_ref)):
            for m in range(part // (2 * HEAD)):
                at = 2 * group * m + 2 * HEAD * (p // 2)
                low, high = ref[:, at : at + 2 * HEAD], ref[:, at + group : at + group + 2 * HEAD]
                if p % 2 == 0:
                    high = jnp.concatenate([high[:, HEAD:], high[:, :HEAD]], axis=1)
                else:
                    low = jnp.concatenate([low[:, HEAD:], low[:, :HEAD]], axis=1)
                to = part * i + 2 * HEAD * m
                buf[p, :, to : to + 2 * HEAD] = jnp.where(lane < HEAD, low, high)
        for i in range(sections):
            buf[p, HEAD * i : HEAD * (i + 1), 3 * part :] = o_ref[
                HEAD * p : HEAD * (p + 1), part * i : part * (i + 1)
            ]
        for half in range(2):
            cut = buf.at[p, :, pl.ds(half * 2 * part, 2 * part)]
            for k in range(sections):

                @pl.when((me ^ k) == p)
                def _(k=k, p=p, cut=cut, half=half):
                    to = outs[sections * half + k]
                    pltpu.make_async_copy(cut, to, sems.at[2 * p + half]).start()

            waits.append(pltpu.make_async_copy(cut, outs[0], sems.at[2 * p + half]))
    for w in waits:
        w.wait()


def pick_body(tables, me_ref, *refs):
    sources, target, sems = refs[:-2], refs[-2], refs[-1]
    width = sources[0].shape[1]
    copies = [
        choose(sources, lookup(table, me_ref[0]), target.at[:, width * i : width * (i + 1)], sems.at[i])
        for i, table in enumerate(tables)
    ]
    for copy in copies:
        copy.wait()


def encoder_rows_body(sections, me_ref, *refs):
    packs, (enc, valid_out, gain_out) = refs[:sections], refs[sections:]
    me = me_ref[0]
    rows = enc.shape[0] // sections
    valid = jnp.zeros((1, enc.shape[0]), F32)
    for k in range(sections):
        enc[pl.ds(pl.multiple_of((me ^ k) * rows, rows), rows), :] = packs[k][:rows, :]
        tail = packs[k][rows : rows + 16, :].astype(F32)
        valid = valid + tail[0:1, : enc.shape[0]]
        gain_out[me ^ k] = jnp.broadcast_to(tail[1:2, :], gain_out.shape[1:])
    valid_out[...] = jnp.broadcast_to(valid, valid_out.shape)


def forward_body(sections, section, source, me_ref, *refs):
    xs, refs = refs[:sections], refs[sections:]
    enc, valid_ref, gain_ref, refs = refs[0], refs[1], refs[2], refs[3:]
    gs, refs = refs[: source.count], refs[source.count :]
    q_out, k_out, prob_out, x_rows, inv_rows, x_buf, w_buf, sems = refs
    me = me_ref[0]
    x_copy = choose(xs, me ^ section, x_buf, sems.at[0])
    part = q_out.shape[1]
    w_copies = [source.load(gs, me, i, part, w_buf.at[i], sems.at[1 + i]) for i in range(2)]
    gain, valid = gain_ref[section, 0:1, :], valid_ref[0:1, :]
    w_copies[1].wait()
    k_out[...] = dot_nn(enc[...], w_buf[1]).astype(BF16)
    x_copy.wait()
    x = x_buf[...].astype(F32)
    inv = lax.rsqrt(jnp.mean(x * x, axis=1, keepdims=True) + 1e-06)
    block = x_rows.shape[0]
    x_mine = x_buf[pl.ds(pl.multiple_of(me * block, block), block), :]
    x_rows[...] = x_mine
    mine = x_mine.astype(F32)
    inv_rows[...] = jnp.broadcast_to(
        lax.rsqrt(jnp.mean(mine * mine, axis=1, keepdims=True) + 1e-06), inv_rows.shape
    )
    x_buf[...] = (x * inv * gain).astype(BF16)
    w_copies[0].wait()
    q_out[...] = dot_nn(x_buf[...], w_buf[0]).astype(BF16)
    lane = lax.broadcasted_iota(jnp.int32, (q_out.shape[0], 2 * HEAD), 1)
    for pair in range(part // (2 * HEAD)):
        cols = slice(2 * HEAD * pair, 2 * HEAD * (pair + 1))
        q, k = q_out[:, cols], k_out[:, cols]
        for h in range(2):
            scores = dot_nt(jnp.where((lane < HEAD) == (h == 0), q, 0), k)
            raw = jnp.exp(scores) * valid
            prob_out[2 * pair + h] = (raw / jnp.sum(raw, axis=1, keepdims=True)).astype(BF16)


class Source:
    def __init__(self, arrays, places, table):
        self.arrays, self.places, self.table = arrays, places, table
        self.count = len(arrays)

    def load(self, refs, me, i, part, target, sem):
        views = [refs[a].at[:, part * (2 * h + i) : part * (2 * h + i + 1)] for a, h in self.places]
        return choose(views, lookup(self.table, me), target, sem)


def lookup(table, me):
    value = jnp.int32(table[0])
    for i in range(1, len(table)):
        value = jnp.where(me == i, jnp.int32(table[i]), value)
    return value


def chain_body(sections, first, second, whole, me_ref, *refs):
    grads, refs = (refs[:1], refs[1:]) if whole else (refs[:sections], refs[sections:])
    g1, refs = refs[: first.count], refs[first.count :]
    g2, refs = refs[: second.count], refs[second.count :]
    k_ref, enc, prob_ref = refs[:3]
    outs, refs = refs[3 : 3 + sections], refs[3 + sections :]
    score_out, attn_out, grad, v_ref, gq, total, w_buf, sems = refs
    me = me_ref[0]
    part = k_ref.shape[1]
    v_copy = second.load(g2, me, 0, part, w_buf.at[2], sems.at[2])
    o_copy = second.load(g2, me, 1, part, w_buf.at[0], sems.at[0])
    q_copy = first.load(g1, me, 0, part, w_buf.at[1], sems.at[1])
    block = total.shape[0] // sections
    if whole:
        grad = grads[0]
    else:
        for k in range(sections):
            grad[pl.ds(pl.multiple_of((me ^ k) * block, block), block), :] = grads[k][...]
    v_copy.wait()
    v_ref[...] = dot_nn(enc[...], w_buf[2]).astype(BF16)
    o_copy.wait()
    ranks = part // HEAD
    attn = jnp.zeros((grad.shape[0], part), F32)
    for i in range(sections):
        weight = jnp.concatenate(
            [
                w_buf[0, (sections * r + i) * HEAD : (sections * r + i + 1) * HEAD, :]
                for r in range(ranks)
            ]
        )
        attn = attn + dot_nt(grad[:, part * i : part * (i + 1)], weight)
    attn_out[...] = attn.astype(BF16)
    lane = lax.broadcasted_iota(jnp.int32, (attn_out.shape[0], 2 * HEAD), 1)
    for pair in range(part // (2 * HEAD)):
        cols = slice(2 * HEAD * pair, 2 * HEAD * (pair + 1))
        a, v, k = attn_out[:, cols], v_ref[:, cols], k_ref[:, cols]
        got = []
        for h in range(2):
            grad_prob = dot_nt(jnp.where((lane < HEAD) == (h == 0), a, 0), v)
            prob = prob_ref[2 * pair + h].astype(F32)
            inner = jnp.sum(prob * grad_prob, axis=1, keepdims=True)
            score = (prob * (grad_prob - inner)).astype(BF16)
            score_out[2 * pair + h] = score
            got.append(dot_nn(score, k))
        gq[:, cols] = jnp.where(lane < HEAD, got[0], got[1]).astype(BF16)
    q_copy.wait()
    total[...] = dot_nt(gq[...], w_buf[1]).astype(BF16)
    for j in range(sections):
        outs[j][...] = total[pl.ds(pl.multiple_of((me ^ j) * block, block), block), :]


def encoder_body(sections, one, two, first, last, me_ref, *refs):
    g1, refs = refs[: one.count], refs[one.count :]
    g2, refs = refs[: two.count], refs[two.count :]
    score_ref, prob_ref, attn_ref, q_ref = refs[:4]
    refs = refs[4:]
    if not first:
        acc_in, refs = refs[0], refs[1:]
    if last:
        outs, refs = refs[:sections], refs[sections:]
    else:
        acc_out, refs = refs[0], refs[1:]
    gk, gv, total, w_buf, sems = refs
    me = me_ref[0]
    part = q_ref.shape[1]
    copies = [
        one.load(g1, me, 1, part, w_buf.at[0], sems.at[0]),
        two.load(g2, me, 0, part, w_buf.at[1], sems.at[1]),
    ]
    lane = lax.broadcasted_iota(jnp.int32, (q_ref.shape[0], 2 * HEAD), 1)

    @pl.loop(0, part // (2 * HEAD))
    def _(pair):
        cols = pl.ds(pl.multiple_of(2 * HEAD * pair, 2 * HEAD), 2 * HEAD)
        a, q = attn_ref[:, cols], q_ref[:, cols]
        ks = [dot_tn(score_ref[2 * pair + h], q) for h in range(2)]
        vs = [dot_tn(prob_ref[2 * pair + h], a) for h in range(2)]
        gk[:, cols] = jnp.where(lane < HEAD, ks[0], ks[1]).astype(BF16)
        gv[:, cols] = jnp.where(lane < HEAD, vs[0], vs[1]).astype(BF16)
    for c in copies:
        c.wait()
    value = dot_nt(gk[...], w_buf[0]) + dot_nt(gv[...], w_buf[1])
    if not first:
        value = value + acc_in[...]
    if not last:
        acc_out[...] = value
    else:
        total[...] = value.astype(BF16)
        block = total.shape[0] // sections
        for j in range(sections):
            outs[j][...] = total[pl.ds(pl.multiple_of((me ^ j) * block, block), block), :]


def finish_body(count, section, me_ref, *refs):
    terms, refs = refs[:4], refs[4:]
    grads, refs = refs[:count], refs[count:]
    x_ref, inv_ref, gain_ref, out = refs
    total = terms[0][...].astype(F32)
    for t in terms[1:]:
        total = total + t[...].astype(F32)
    scaled = gain_ref[section, 0:1, :] * total
    x, inv = x_ref[...].astype(F32), inv_ref[:, 0:1]
    branch = inv * scaled - x * inv * inv * inv * jnp.mean(x * scaled, axis=1, keepdims=True)
    block = out.shape[0]
    me = me_ref[0]
    if grads[0].shape[0] == block:
        grad = grads[0][...]
    else:
        grad = grads[0][pl.ds(pl.multiple_of(me * block, block), block), :]
    out[...] = (grad.astype(F32) + branch).astype(BF16)


def head_device(
    hidden_in, grad_out, encoder_out, enc_valid, norm_gain, w_query, w_key, w_value, w_out
):
    sections = lax.axis_size("section")
    ranks = lax.axis_size("dp")
    levels = ranks // CORES
    me = lax.axis_index("section")
    me_ref = jnp.reshape(me, (1,)).astype(jnp.int32)
    axes = ("section", "dp")
    shard, inner = w_query.shape[1], w_query.shape[2]
    width = hidden_in.shape[3]
    dec_rows = hidden_in.shape[2]
    enc_rows = encoder_out.shape[1]
    part = inner // sections
    heads = part // HEAD
    block = dec_rows // sections
    keys = enc_rows * sections

    def peer(array, k, targets):
        pairs = [((s ^ k) * ranks + r, s * ranks + r) for s in targets for r in range(ranks)]
        return lax.ppermute(array, axes, pairs)

    def peers(arrays, targets=range(sections)):
        return [arrays[0]] + [peer(arrays[k], k, targets) for k in range(1, sections)]

    def shape(dims, dtype=BF16):
        return jax.ShapeDtypeStruct(dims, dtype)

    pieces = call(
        functools.partial(pieces_body, sections),
        [shape((shard, 2 * part))] * (2 * sections),
        [me_ref, w_query[0], w_key[0], w_value[0], w_out[0]],
        [SMEM] + [VMEM] * 4,
        [pltpu.VMEM((sections, shard, inner), BF16), pltpu.SemaphoreType.DMA((2 * sections,))],
        0,
        8 * shard * inner * sections,
        out_specs=[ANY] * (2 * sections),
    )
    valid_row = lax.dynamic_update_slice(
        jnp.zeros((1, width), BF16), enc_valid.astype(BF16), (0, me * enc_rows)
    )
    pack = jnp.concatenate([encoder_out[0], valid_row, norm_gain, jnp.zeros((14, width), BF16)])
    arrived = [peers(pieces[:sections]), peers(pieces[sections:])]
    packs = peers([pack] * sections)
    hidden = peers([hidden_in[0, 0]] * sections)
    encoded, valid, gains = call(
        functools.partial(encoder_rows_body, sections),
        [shape((keys, width)), shape((8, keys), F32), shape((sections, 8, width), F32)],
        [me_ref] + packs,
        [SMEM] + [VMEM] * sections,
        [],
        0,
        4 * keys * width,
    )

    order = [
        [(i, 0)]
        + [(s, h) for s in reversed(range(sections)) for h in range(2) if (s, h) != (i, 0)]
        for i in range(sections)
    ]
    spans = [(0, 1), (1, 2 * sections - 3), (2 * sections - 3, 2 * sections - 1)]
    spans += [(2 * sections - 1, 2 * sections)]
    held = []
    for low, high in spans:
        wanted = [
            [(i ^ order[i][turn][0], order[i][turn][1]) for i in range(sections)]
            for turn in range(low, high)
        ]
        unique = sorted(set(sum(wanted, [])))
        options = [arrived[h][k] for k, h in unique]
        if len(options) > 1:
            tables = [[unique.index(w) for w in want] for want in wanted]
            value = call(
                functools.partial(pick_body, tables),
                [shape((shard, options[0].shape[1] * (high - low)))],
                [me_ref] + options,
                [SMEM] + [ANY] * len(options),
                [pltpu.SemaphoreType.DMA((high - low,))],
                0,
                4 * options[0].size * (high - low),
            )[0]
        else:
            value = options[0]
        held.append(lax.all_gather(value, "dp", axis=0, tiled=True))
    place = {t: (j, t - low) for j, (low, high) in enumerate(spans) for t in range(low, high)}

    def source(s, h):
        found = [place[order[i].index((s, h))] for i in range(sections)]
        places = sorted(set(found))
        arrays = sorted({j for j, _ in places})
        return Source(
            [held[j] for j in arrays],
            [(arrays.index(j), at) for j, at in places],
            [places.index(f) for f in found],
        )

    gemm = 2 * dec_rows * width * part
    rows_spec = shape((block, width))
    halves = [(source(s, 0), source(s, 1)) for s in range(sections)]

    def forward(s, after):
        one = halves[s][0]
        return call(
            functools.partial(forward_body, sections, s, one),
            [shape((dec_rows, part)), shape((keys, part))]
            + [shape((heads, dec_rows, keys)), rows_spec, shape((block, 128), F32)],
            [me_ref] + hidden + [encoded, valid, gains] + one.arrays,
            [SMEM] + [ANY] * sections + [VMEM] * 3 + [ANY] * one.count,
            [
                pltpu.VMEM((dec_rows, width), BF16),
                pltpu.VMEM((2, width, part), BF16),
                pltpu.SemaphoreType.DMA((3,)),
            ],
            2 * gemm,
            8 * width * part,
            after=after,
        )

    def chain(s, grads, k, prob, after):
        one, two = halves[s]
        return call(
            functools.partial(chain_body, sections, one, two, len(grads) == 1),
            [rows_spec] * sections + [shape((heads, dec_rows, keys)), shape((dec_rows, part))],
            [me_ref] + grads + one.arrays + two.arrays + [k, encoded, prob],
            [SMEM] + [VMEM] * len(grads) + [ANY] * (one.count + two.count) + [VMEM] * 3,
            [
                pltpu.VMEM((dec_rows, width), BF16),
                pltpu.VMEM((keys, part), BF16),
                pltpu.VMEM((dec_rows, part), BF16),
                pltpu.VMEM((dec_rows, width), BF16),
                pltpu.VMEM((3, width, part), BF16),
                pltpu.SemaphoreType.DMA((3,)),
            ],
            3 * gemm,
            12 * width * part,
            after=after,
        )

    def encoder(s, score, prob, attn, q, acc, after):
        one, two = halves[s]
        return call(
            functools.partial(encoder_body, sections, one, two, not acc, s == 0),
            [shape((enc_rows, width))] * sections if s == 0 else [shape((keys, width), F32)],
            [me_ref] + one.arrays + two.arrays + [score, prob, attn, q] + acc,
            [SMEM] + [ANY] * (one.count + two.count) + [VMEM] * (4 + len(acc)),
            [
                pltpu.VMEM((keys, part), BF16),
                pltpu.VMEM((keys, part), BF16),
                pltpu.VMEM((keys, width), BF16),
                pltpu.VMEM((2, width, part), BF16),
                pltpu.SemaphoreType.DMA((2,)),
            ],
            2 * gemm,
            8 * width * part,
            after=after,
        )

    grads = [grad_out[0]]
    done, acc, ready = [None] * sections, [], None
    for s in reversed(range(sections)):
        q, k, prob, x_rows, inv_rows = forward(s, acc) if ready is None else ready
        ready = None
        outs = chain(s, grads, k, prob, acc)
        terms, score, attn = peers(outs[:sections]), outs[sections], outs[sections + 1]
        early = []
        if s in (1, sections - 1):
            ready = forward(s - 1, [attn])
            early = [ready[0]]
        if s == 0:
            acc = encoder(s, score, prob, attn, q, acc, [])
            early = [acc[0]]
        mine = call(
            functools.partial(finish_body, 1, s),
            [rows_spec],
            [me_ref] + terms + [grads[0], x_rows, inv_rows, gains],
            [SMEM] + [VMEM] * 8,
            [],
            block * width * 10,
            block * width * 20,
            after=early,
        )[0]
        grads = peers([mine] * sections, range(sections) if s > 0 else (0,))
        done[s] = grads
        if s > 0:
            acc = encoder(s, score, prob, attn, q, acc, [mine])
    enc_terms = peers(acc)

    def sum_body(*refs):
        total = refs[0][...].astype(F32)
        for r in refs[1:-1]:
            total = total + r[...].astype(F32)
        refs[-1][...] = total.astype(BF16)

    enc_grad = call(
        sum_body,
        [shape((enc_rows, width))],
        enc_terms,
        [VMEM] * sections,
        [],
        enc_rows * width * 4,
        enc_rows * width * 10,
    )[0]

    def result_body(me_ref, *refs):
        out, sems = refs[-2], refs[-1]
        me = me_ref[0]
        for k in range(sections):
            at = pl.ds(pl.multiple_of((me ^ k) * block, block), block)
            choose([refs[sections * s + k] for s in range(sections)], me, out.at[at], sems.at[k])
        for k in range(sections):
            at = pl.ds(pl.multiple_of((me ^ k) * block, block), block)
            pltpu.make_async_copy(refs[k], out.at[at], sems.at[k]).wait()

    result = call(
        result_body,
        [shape((dec_rows, width))],
        [me_ref] + [g for s in range(sections) for g in done[s]],
        [SMEM] + [ANY] * (sections * sections),
        [pltpu.SemaphoreType.DMA((sections,))],
        0,
        dec_rows * width * 4,
    )[0]
    return (result[None, None], enc_grad[None])


def solution(mesh):
    in_specs = (
        P("section", "dp", None, None),
        P("dp", None, None),
        P("dp", "section", None),
        P("dp", "section"),
        P("section", None),
        P("section", "dp", None),
        P("section", "dp", None),
        P("section", "dp", None),
        P("section", "dp", None),
    )
    out_specs = (P("section", "dp", None, None), P("dp", "section", None))

    def run(*args):
        per_device = head_device if plan_fits(mesh.shape, args[5].shape[2]) else relay_device
        return jax.shard_map(
            per_device, mesh=mesh, in_specs=in_specs, out_specs=out_specs, check_vma=False
        )(*args)

    return run
```

```python
import functools

import jax
import jax.numpy as jnp
from jax import lax
from jax.experimental import pallas as pl
from jax.experimental.pallas import tpu as pltpu
from jax.sharding import PartitionSpec as P

HEAD = 64


def from_behind(array, axis, by):
    length = lax.axis_size(axis)
    pairs = [(i, i + by) for i in range(length) if 0 <= i + by < length]
    return lax.ppermute(array, axis, pairs)


def times_transposed(left_side, right_side):
    return lax.dot_general(
        left_side, right_side, (((1,), (1,)), ((), ())), preferred_element_type=jnp.float32
    )


def project_keys(encoded, key_weight, value_weight):
    keys_all = jnp.dot(encoded, key_weight, preferred_element_type=jnp.float32).astype(jnp.bfloat16)
    values_all = jnp.dot(encoded, value_weight, preferred_element_type=jnp.float32).astype(
        jnp.bfloat16
    )
    return (keys_all, values_all)


def relay_device(
    hidden_in, grad_out, encoder_out, enc_valid, norm_gain, w_query, w_key, w_value, w_out
):
    section_count = lax.axis_size("section")
    my_section = lax.axis_index("section")
    valid_half = enc_valid.astype(jnp.bfloat16)
    encoded_all, valid_all = (
        lax.all_gather(encoder_out, "section", axis=1, tiled=True),
        lax.all_gather(valid_half, "section", axis=1, tiled=True),
    )
    encoded = encoded_all[0]
    valid_keys = valid_all[0].astype(jnp.float32)
    query_full, key_full, value_full, out_full = (
        lax.all_gather(w_query, "dp", axis=1, tiled=True),
        lax.all_gather(w_key, "dp", axis=1, tiled=True),
        lax.all_gather(w_value, "dp", axis=1, tiled=True),
        lax.all_gather(w_out, "dp", axis=1, tiled=True),
    )
    keys_all, values_all = project_keys(encoded, key_full[0], value_full[0])
    query_weight = query_full[0]
    key_weight = key_full[0]
    value_weight = value_full[0]
    out_weight = out_full[0]
    dec_rows, width = (hidden_in.shape[2], hidden_in.shape[3])
    enc_rows = encoded.shape[0]
    inner_width = query_weight.shape[1]
    head_count = inner_width // HEAD
    in_float = hidden_in[0, 0].astype(jnp.float32)
    gain_row = norm_gain[0].astype(jnp.float32)
    inv_rms = lax.rsqrt(jnp.mean(in_float * in_float, axis=1, keepdims=True) + 1e-06)
    normed = (in_float * inv_rms * gain_row).astype(jnp.bfloat16)
    queries = jnp.dot(normed, query_weight, preferred_element_type=jnp.float32).astype(jnp.bfloat16)
    query_heads = queries.reshape(dec_rows, head_count, HEAD)
    key_heads = keys_all.reshape(enc_rows, head_count, HEAD)
    value_heads = values_all.reshape(enc_rows, head_count, HEAD)
    scores = jnp.einsum("lhd,ehd->hle", query_heads, key_heads, preferred_element_type=jnp.float32)
    raw = jnp.exp(scores) * valid_keys[None, None, :]
    attn_prob = raw / jnp.sum(raw, axis=2, keepdims=True)
    prob_half = attn_prob.astype(jnp.bfloat16)

    def backward_step(grad_y):
        grad_attn = times_transposed(grad_y, out_weight).astype(jnp.bfloat16)
        attn_heads = grad_attn.reshape(dec_rows, head_count, HEAD)
        grad_prob = jnp.einsum(
            "lhd,ehd->hle", attn_heads, value_heads, preferred_element_type=jnp.float32
        )
        inner_sum = jnp.sum(attn_prob * grad_prob, axis=2, keepdims=True)
        grad_scores = (attn_prob * (grad_prob - inner_sum)).astype(jnp.bfloat16)
        grad_query = jnp.einsum(
            "hle,ehd->lhd", grad_scores, key_heads, preferred_element_type=jnp.float32
        ).astype(jnp.bfloat16)
        grad_key = jnp.einsum(
            "hle,lhd->ehd", grad_scores, query_heads, preferred_element_type=jnp.float32
        ).astype(jnp.bfloat16)
        grad_value = jnp.einsum(
            "hle,lhd->ehd", prob_half, attn_heads, preferred_element_type=jnp.float32
        ).astype(jnp.bfloat16)
        grad_normed = times_transposed(grad_query.reshape(dec_rows, inner_width), query_weight)
        scaled_grad = gain_row * grad_normed
        branch = inv_rms * scaled_grad - in_float * inv_rms * inv_rms * inv_rms * jnp.mean(
            in_float * scaled_grad, axis=1, keepdims=True
        )
        grad_input = (grad_y.astype(jnp.float32) + branch).astype(jnp.bfloat16)
        return (
            grad_input,
            grad_key.reshape(enc_rows, inner_width),
            grad_value.reshape(enc_rows, inner_width),
        )

    zero_input = jnp.zeros((dec_rows, width), jnp.bfloat16)
    zero_enc = jnp.zeros((enc_rows, inner_width), jnp.bfloat16)

    def loop_body(step_index, state_now):
        grad_now, grad_done, key_grad, value_grad = state_now
        is_active = my_section == section_count - 1 - step_index
        grad_done, key_grad, value_grad = lax.cond(
            is_active, lambda: backward_step(grad_now), lambda: (grad_done, key_grad, value_grad)
        )
        grad_now = from_behind(grad_done, "section", -1)
        return (grad_now, grad_done, key_grad, value_grad)

    grad_now, grad_done, key_grad, value_grad = lax.fori_loop(
        0, section_count - 1, loop_body, (grad_out[0], zero_input, zero_enc, zero_enc)
    )
    grad_done, key_grad, value_grad = lax.cond(
        my_section == 0, lambda: backward_step(grad_now), lambda: (grad_done, key_grad, value_grad)
    )
    enc_grad = lax.psum_scatter(
        (
            times_transposed(key_grad, key_weight) + times_transposed(value_grad, value_weight)
        ).astype(jnp.bfloat16),
        "section",
        scatter_dimension=0,
        tiled=True,
    )
    return (grad_done[None, None], enc_grad[None])

CORES = 2
ANY = pl.BlockSpec(memory_space=pl.ANY)
SMEM = pl.BlockSpec(memory_space=pltpu.SMEM)
VMEM = pl.BlockSpec(memory_space=pltpu.VMEM)
F32, BF16 = jnp.float32, jnp.bfloat16


def plan_fits(mesh_shape, dims):
    sections, ranks = mesh_shape["section"], mesh_shape["dp"]
    return sections == 4 and dims == ranks * sections * HEAD and ranks == 8


def dot_nt(a, b):
    return lax.dot_general(a, b, (((1,), (1,)), ((), ())), preferred_element_type=F32)


def dot_tn(a, b):
    return lax.dot_general(a, b, (((0,), (0,)), ((), ())), preferred_element_type=F32)


def dot_nn(a, b):
    return jnp.dot(a, b, preferred_element_type=F32)


def call(body, outs, inputs, specs, scratch, flops, size, out_specs=None, after=()):
    count = len(inputs)

    def kernel(*refs):
        body(*refs[:count], *refs[count + len(after) :])

    return list(pl.pallas_call(
        kernel,
        out_shape=outs,
        in_specs=specs + [ANY] * len(after),
        out_specs=[VMEM] * len(outs) if out_specs is None else out_specs,
        scratch_shapes=scratch,
        cost_estimate=pl.CostEstimate(flops=flops, bytes_accessed=size, transcendentals=0),
        compiler_params=pltpu.CompilerParams(vmem_limit_bytes=56 * 2**20),
    )(*inputs, *after))


def choose(sources, index, target, sem):
    if len(sources) == 1:
        copy = pltpu.make_async_copy(sources[0], target, sem)
        copy.start()
        return copy
    for i, source in enumerate(sources):

        @pl.when(index == i)
        def _(source=source):
            pltpu.make_async_copy(source, target, sem).start()

    return pltpu.make_async_copy(sources[0], target, sem)


def pieces_body(sections, half, me_ref, first_ref, second_ref, *rest):
    outs, buf, sems = rest[:sections], rest[sections], rest[sections + 1]
    me = me_ref[0]
    rows, inner = first_ref.shape
    part = inner // sections
    group = sections * HEAD
    lane = lax.broadcasted_iota(jnp.int32, (rows, 2 * HEAD), 1)
    waits = []
    for p in range(sections):
        for i, ref in enumerate((first_ref, second_ref) if half == 0 else (first_ref,)):
            for m in range(part // (2 * HEAD)):
                at = 2 * group * m + 2 * HEAD * (p // 2)
                low, high = ref[:, at : at + 2 * HEAD], ref[:, at + group : at + group + 2 * HEAD]
                if p % 2 == 0:
                    high = jnp.concatenate([high[:, HEAD:], high[:, :HEAD]], axis=1)
                else:
                    low = jnp.concatenate([low[:, HEAD:], low[:, :HEAD]], axis=1)
                to = part * i + 2 * HEAD * m
                buf[p, :, to : to + 2 * HEAD] = jnp.where(lane < HEAD, low, high)
        if half == 1:
            for i in range(sections):
                buf[p, HEAD * i : HEAD * (i + 1), part:] = second_ref[
                    HEAD * p : HEAD * (p + 1), part * i : part * (i + 1)
                ]
        for k in range(sections):

            @pl.when((me ^ k) == p)
            def _(k=k, p=p):
                pltpu.make_async_copy(buf.at[p], outs[k], sems.at[p]).start()

        waits.append(pltpu.make_async_copy(buf.at[p], outs[0], sems.at[p]))
    for w in waits:
        w.wait()


def pick_body(tables, me_ref, *refs):
    sources, (target, buf, sems) = refs[:-3], refs[-3:]
    width = sources[0].shape[1]
    copies = [
        choose(sources, lookup(table, me_ref[0]), buf.at[i], sems.at[i])
        for i, table in enumerate(tables)
    ]
    outs = []
    for i, copy in enumerate(copies):
        copy.wait()
        to = target.at[:, width * i : width * (i + 1)]
        outs.append(pltpu.make_async_copy(buf.at[i], to, sems.at[len(tables) + i]))
        outs[-1].start()
    for out in outs:
        out.wait()


def encoder_rows_body(sections, me_ref, *refs):
    packs, (enc, valid_out, gain_out) = refs[:sections], refs[sections:]
    me = me_ref[0]
    rows = enc.shape[0] // sections
    valid = jnp.zeros((1, enc.shape[0]), F32)
    for k in range(sections):
        enc[pl.ds(pl.multiple_of((me ^ k) * rows, rows), rows), :] = packs[k][:rows, :]
        tail = packs[k][rows : rows + 16, :].astype(F32)
        valid = valid + tail[0:1, : enc.shape[0]]
        gain_out[me ^ k] = jnp.broadcast_to(tail[1:2, :], gain_out.shape[1:])
    valid_out[...] = jnp.broadcast_to(valid, valid_out.shape)


def forward_body(sections, section, source, me_ref, *refs):
    xs, refs = refs[:sections], refs[sections:]
    enc, valid_ref, gain_ref, refs = refs[0], refs[1], refs[2], refs[3:]
    gs, refs = refs[: source.count], refs[source.count :]
    q_out, k_out, prob_out, x_rows, inv_rows, x_buf, w_buf, sems = refs
    me = me_ref[0]
    x_copy = choose(xs, me ^ section, x_buf, sems.at[0])
    part = q_out.shape[1]
    w_copies = [source.load(gs, me, i, part, w_buf.at[i], sems.at[1 + i]) for i in range(2)]
    gain, valid = gain_ref[section, 0:1, :], valid_ref[0:1, :]
    w_copies[1].wait()
    k_out[...] = dot_nn(enc[...], w_buf[1]).astype(BF16)
    x_copy.wait()
    x = x_buf[...].astype(F32)
    inv = lax.rsqrt(jnp.mean(x * x, axis=1, keepdims=True) + 1e-06)
    block = x_rows.shape[0]
    x_mine = x_buf[pl.ds(pl.multiple_of(me * block, block), block), :]
    x_rows[...] = x_mine
    mine = x_mine.astype(F32)
    inv_rows[...] = jnp.broadcast_to(
        lax.rsqrt(jnp.mean(mine * mine, axis=1, keepdims=True) + 1e-06), inv_rows.shape
    )
    x_buf[...] = (x * inv * gain).astype(BF16)
    w_copies[0].wait()
    q_out[...] = dot_nn(x_buf[...], w_buf[0]).astype(BF16)
    lane = lax.broadcasted_iota(jnp.int32, (q_out.shape[0], 2 * HEAD), 1)
    for pair in range(part // (2 * HEAD)):
        cols = slice(2 * HEAD * pair, 2 * HEAD * (pair + 1))
        q, k = q_out[:, cols], k_out[:, cols]
        for h in range(2):
            scores = dot_nt(jnp.where((lane < HEAD) == (h == 0), q, 0), k)
            raw = jnp.exp(scores) * valid
            prob_out[2 * pair + h] = (raw / jnp.sum(raw, axis=1, keepdims=True)).astype(BF16)


class Source:
    def __init__(self, arrays, places, table):
        self.arrays, self.places, self.table = arrays, places, table
        self.count = len(arrays)

    def load(self, refs, me, i, part, target, sem):
        views = [refs[a].at[:, part * (2 * h + i) : part * (2 * h + i + 1)] for a, h in self.places]
        return choose(views, lookup(self.table, me), target, sem)


def lookup(table, me):
    value = jnp.int32(table[0])
    for i in range(1, len(table)):
        value = jnp.where(me == i, jnp.int32(table[i]), value)
    return value


def chain_body(sections, first, second, whole, me_ref, *refs):
    grads, refs = (refs[:1], refs[1:]) if whole else (refs[:sections], refs[sections:])
    g1, refs = refs[: first.count], refs[first.count :]
    g2, refs = refs[: second.count], refs[second.count :]
    k_ref, enc, prob_ref = refs[:3]
    outs, refs = refs[3 : 3 + sections], refs[3 + sections :]
    score_out, attn_out, grad, v_ref, gq, total, w_buf, sems = refs
    me = me_ref[0]
    part = k_ref.shape[1]
    v_copy = second.load(g2, me, 0, part, w_buf.at[2], sems.at[2])
    o_copy = second.load(g2, me, 1, part, w_buf.at[0], sems.at[0])
    q_copy = first.load(g1, me, 0, part, w_buf.at[1], sems.at[1])
    block = total.shape[0] // sections
    if whole:
        grad = grads[0]
    else:
        rows_in = []
        for k in range(sections):
            to = grad.at[pl.ds(pl.multiple_of((me ^ k) * block, block), block), :]
            rows_in.append(pltpu.make_async_copy(grads[k], to, sems.at[3 + k]))
            rows_in[-1].start()
    v_copy.wait()
    v_ref[...] = dot_nn(enc[...], w_buf[2]).astype(BF16)
    if not whole:
        for copy in rows_in:
            copy.wait()
    o_copy.wait()
    ranks = part // HEAD
    attn = jnp.zeros((grad.shape[0], part), F32)
    for i in range(sections):
        weight = jnp.concatenate(
            [
                w_buf[0, (sections * r + i) * HEAD : (sections * r + i + 1) * HEAD, :]
                for r in range(ranks)
            ]
        )
        attn = attn + dot_nt(grad[:, part * i : part * (i + 1)], weight)
    attn_out[...] = attn.astype(BF16)
    lane = lax.broadcasted_iota(jnp.int32, (attn_out.shape[0], 2 * HEAD), 1)
    for pair in range(part // (2 * HEAD)):
        cols = slice(2 * HEAD * pair, 2 * HEAD * (pair + 1))
        a, v, k = attn_out[:, cols], v_ref[:, cols], k_ref[:, cols]
        got = []
        for h in range(2):
            grad_prob = dot_nt(jnp.where((lane < HEAD) == (h == 0), a, 0), v)
            prob = prob_ref[2 * pair + h].astype(F32)
            inner = jnp.sum(prob * grad_prob, axis=1, keepdims=True)
            score = (prob * (grad_prob - inner)).astype(BF16)
            score_out[2 * pair + h] = score
            got.append(dot_nn(score, k))
        gq[:, cols] = jnp.where(lane < HEAD, got[0], got[1]).astype(BF16)
    q_copy.wait()
    total[...] = dot_nt(gq[...], w_buf[1]).astype(BF16)
    for j in range(sections):
        outs[j][...] = total[pl.ds(pl.multiple_of((me ^ j) * block, block), block), :]


def encoder_body(sections, one, two, first, last, me_ref, *refs):
    g1, refs = refs[: one.count], refs[one.count :]
    g2, refs = refs[: two.count], refs[two.count :]
    score_ref, prob_ref, attn_ref, q_ref = refs[:4]
    refs = refs[4:]
    if not first:
        acc_in, refs = refs[0], refs[1:]
    if last:
        outs, refs = refs[:sections], refs[sections:]
    else:
        acc_out, refs = refs[0], refs[1:]
    gk, gv, total, w_buf, sems = refs
    me = me_ref[0]
    part = q_ref.shape[1]
    copies = [
        one.load(g1, me, 1, part, w_buf.at[0], sems.at[0]),
        two.load(g2, me, 0, part, w_buf.at[1], sems.at[1]),
    ]
    lane = lax.broadcasted_iota(jnp.int32, (q_ref.shape[0], 2 * HEAD), 1)

    @pl.loop(0, part // (2 * HEAD))
    def _(pair):
        cols = pl.ds(pl.multiple_of(2 * HEAD * pair, 2 * HEAD), 2 * HEAD)
        a, q = attn_ref[:, cols], q_ref[:, cols]
        ks = [dot_tn(score_ref[2 * pair + h], q) for h in range(2)]
        vs = [dot_tn(prob_ref[2 * pair + h], a) for h in range(2)]
        gk[:, cols] = jnp.where(lane < HEAD, ks[0], ks[1]).astype(BF16)
        gv[:, cols] = jnp.where(lane < HEAD, vs[0], vs[1]).astype(BF16)
    for c in copies:
        c.wait()
    value = dot_nt(gk[...], w_buf[0]) + dot_nt(gv[...], w_buf[1])
    if not first:
        value = value + acc_in[...]
    if not last:
        acc_out[...] = value
    else:
        total[...] = value.astype(BF16)
        block = total.shape[0] // sections
        for j in range(sections):
            outs[j][...] = total[pl.ds(pl.multiple_of((me ^ j) * block, block), block), :]


def finish_body(count, section, me_ref, *refs):
    terms, refs = refs[:4], refs[4:]
    grads, refs = refs[:count], refs[count:]
    x_ref, inv_ref, gain_ref, out = refs
    total = terms[0][...].astype(F32)
    for t in terms[1:]:
        total = total + t[...].astype(F32)
    scaled = gain_ref[section, 0:1, :] * total
    x, inv = x_ref[...].astype(F32), inv_ref[:, 0:1]
    branch = inv * scaled - x * inv * inv * inv * jnp.mean(x * scaled, axis=1, keepdims=True)
    block = out.shape[0]
    me = me_ref[0]
    if grads[0].shape[0] == block:
        grad = grads[0][...]
    else:
        grad = grads[0][pl.ds(pl.multiple_of(me * block, block), block), :]
    out[...] = (grad.astype(F32) + branch).astype(BF16)


def head_device(
    hidden_in, grad_out, encoder_out, enc_valid, norm_gain, w_query, w_key, w_value, w_out
):
    sections = lax.axis_size("section")
    ranks = lax.axis_size("dp")
    levels = ranks // CORES
    me = lax.axis_index("section")
    me_ref = jnp.reshape(me, (1,)).astype(jnp.int32)
    axes = ("section", "dp")
    shard, inner = w_query.shape[1], w_query.shape[2]
    width = hidden_in.shape[3]
    dec_rows = hidden_in.shape[2]
    enc_rows = encoder_out.shape[1]
    part = inner // sections
    heads = part // HEAD
    block = dec_rows // sections
    keys = enc_rows * sections

    def peer(array, k, targets):
        pairs = [((s ^ k) * ranks + r, s * ranks + r) for s in targets for r in range(ranks)]
        return lax.ppermute(array, axes, pairs)

    def peers(arrays, targets=range(sections)):
        return [arrays[0]] + [peer(arrays[k], k, targets) for k in range(1, sections)]

    def shape(dims, dtype=BF16):
        return jax.ShapeDtypeStruct(dims, dtype)

    def cut_pieces(half, first, second, after):
        return call(
            functools.partial(pieces_body, sections, half),
            [shape((shard, 2 * part))] * sections,
            [me_ref, first[0], second[0]],
            [SMEM, VMEM, VMEM],
            [pltpu.VMEM((sections, shard, 2 * part), BF16), pltpu.SemaphoreType.DMA((sections,))],
            0,
            4 * shard * inner * sections,
            out_specs=[ANY] * sections,
            after=after,
        )

    arrived = [peers(cut_pieces(0, w_query, w_key, []))]
    arrived.append(peers(cut_pieces(1, w_value, w_out, arrived[0][1:2])))
    valid_row = lax.dynamic_update_slice(
        jnp.zeros((1, width), BF16), enc_valid.astype(BF16), (0, me * enc_rows)
    )
    pack = jnp.concatenate([encoder_out[0], valid_row, norm_gain, jnp.zeros((14, width), BF16)])
    packs = peers([pack] * sections)
    hidden = peers([hidden_in[0, 0]] * sections)
    encoded, valid, gains = call(
        functools.partial(encoder_rows_body, sections),
        [shape((keys, width)), shape((8, keys), F32), shape((sections, 8, width), F32)],
        [me_ref] + packs,
        [SMEM] + [VMEM] * sections,
        [],
        0,
        4 * keys * width,
    )

    order = [
        [(i, 0)]
        + [(s, h) for s in reversed(range(sections)) for h in range(2) if (s, h) != (i, 0)]
        for i in range(sections)
    ]
    spans = [(0, 1), (1, 2 * sections - 3), (2 * sections - 3, 2 * sections - 1)]
    spans += [(2 * sections - 1, 2 * sections)]
    held = []
    for low, high in spans:
        wanted = [
            [(i ^ order[i][turn][0], order[i][turn][1]) for i in range(sections)]
            for turn in range(low, high)
        ]
        unique = sorted(set(sum(wanted, [])))
        options = [arrived[h][k] for k, h in unique]
        if len(options) > 1:
            tables = [[unique.index(w) for w in want] for want in wanted]
            value = call(
                functools.partial(pick_body, tables),
                [shape((shard, options[0].shape[1] * (high - low)))],
                [me_ref] + options,
                [SMEM] + [ANY] * len(options),
                [
                    pltpu.VMEM((high - low,) + options[0].shape, BF16),
                    pltpu.SemaphoreType.DMA((2 * (high - low),)),
                ],
                0,
                4 * options[0].size * (high - low),
                out_specs=[ANY],
            )[0]
        else:
            value = options[0]
        held.append(lax.all_gather(value, "dp", axis=0, tiled=True))
    place = {t: (j, t - low) for j, (low, high) in enumerate(spans) for t in range(low, high)}

    def source(s, h):
        found = [place[order[i].index((s, h))] for i in range(sections)]
        places = sorted(set(found))
        arrays = sorted({j for j, _ in places})
        return Source(
            [held[j] for j in arrays],
            [(arrays.index(j), at) for j, at in places],
            [places.index(f) for f in found],
        )

    gemm = 2 * dec_rows * width * part
    rows_spec = shape((block, width))
    halves = [(source(s, 0), source(s, 1)) for s in range(sections)]

    def forward(s, after):
        one = halves[s][0]
        return call(
            functools.partial(forward_body, sections, s, one),
            [shape((dec_rows, part)), shape((keys, part))]
            + [shape((heads, dec_rows, keys)), rows_spec, shape((block, 128), F32)],
            [me_ref] + hidden + [encoded, valid, gains] + one.arrays,
            [SMEM] + [ANY] * sections + [VMEM] * 3 + [ANY] * one.count,
            [
                pltpu.VMEM((dec_rows, width), BF16),
                pltpu.VMEM((2, width, part), BF16),
                pltpu.SemaphoreType.DMA((3,)),
            ],
            2 * gemm,
            8 * width * part,
            after=after,
        )

    def chain(s, grads, k, prob, after):
        one, two = halves[s]
        return call(
            functools.partial(chain_body, sections, one, two, len(grads) == 1),
            [rows_spec] * sections + [shape((heads, dec_rows, keys)), shape((dec_rows, part))],
            [me_ref] + grads + one.arrays + two.arrays + [k, encoded, prob],
            [SMEM]
            + [VMEM if len(grads) == 1 else ANY] * len(grads)
            + [ANY] * (one.count + two.count)
            + [VMEM] * 3,
            [
                pltpu.VMEM((dec_rows, width), BF16),
                pltpu.VMEM((keys, part), BF16),
                pltpu.VMEM((dec_rows, part), BF16),
                pltpu.VMEM((dec_rows, width), BF16),
                pltpu.VMEM((3, width, part), BF16),
                pltpu.SemaphoreType.DMA((3 + sections,)),
            ],
            3 * gemm,
            12 * width * part,
            after=after,
        )

    def encoder(s, score, prob, attn, q, acc, after):
        one, two = halves[s]
        return call(
            functools.partial(encoder_body, sections, one, two, not acc, s == 0),
            [shape((enc_rows, width))] * sections if s == 0 else [shape((keys, width), F32)],
            [me_ref] + one.arrays + two.arrays + [score, prob, attn, q] + acc,
            [SMEM] + [ANY] * (one.count + two.count) + [VMEM] * (4 + len(acc)),
            [
                pltpu.VMEM((keys, part), BF16),
                pltpu.VMEM((keys, part), BF16),
                pltpu.VMEM((keys, width), BF16),
                pltpu.VMEM((2, width, part), BF16),
                pltpu.SemaphoreType.DMA((2,)),
            ],
            2 * gemm,
            8 * width * part,
            after=after,
        )

    grads = [grad_out[0]]
    done, acc, ready = [None] * sections, [], None
    for s in reversed(range(sections)):
        q, k, prob, x_rows, inv_rows = forward(s, acc) if ready is None else ready
        ready = None
        outs = chain(s, grads, k, prob, acc)
        terms, score, attn = peers(outs[:sections]), outs[sections], outs[sections + 1]
        early = []
        if s in (1, sections - 1):
            ready = forward(s - 1, [attn])
            early = [ready[0]]
        if s == 0:
            acc = encoder(s, score, prob, attn, q, acc, [])
            early = [acc[0]]
        mine = call(
            functools.partial(finish_body, 1, s),
            [rows_spec],
            [me_ref] + terms + [grads[0], x_rows, inv_rows, gains],
            [SMEM] + [VMEM] * 8,
            [],
            block * width * 10,
            block * width * 20,
            after=early,
        )[0]
        grads = peers([mine] * sections, range(sections) if s > 0 else (0,))
        done[s] = grads
        if s > 0:
            acc = encoder(s, score, prob, attn, q, acc, [mine])
    enc_terms = peers(acc)

    def sum_body(*refs):
        total = refs[0][...].astype(F32)
        for r in refs[1:-1]:
            total = total + r[...].astype(F32)
        refs[-1][...] = total.astype(BF16)

    enc_grad = call(
        sum_body,
        [shape((enc_rows, width))],
        enc_terms,
        [VMEM] * sections,
        [],
        enc_rows * width * 4,
        enc_rows * width * 10,
    )[0]

    def result_body(me_ref, *refs):
        out, sems = refs[-2], refs[-1]
        me = me_ref[0]
        for k in range(sections):
            at = pl.ds(pl.multiple_of((me ^ k) * block, block), block)
            choose([refs[sections * s + k] for s in range(sections)], me, out.at[at], sems.at[k])
        for k in range(sections):
            at = pl.ds(pl.multiple_of((me ^ k) * block, block), block)
            pltpu.make_async_copy(refs[k], out.at[at], sems.at[k]).wait()

    result = call(
        result_body,
        [shape((dec_rows, width))],
        [me_ref] + [g for s in range(sections) for g in done[s]],
        [SMEM] + [ANY] * (sections * sections),
        [pltpu.SemaphoreType.DMA((sections,))],
        0,
        dec_rows * width * 4,
    )[0]
    return (result[None, None], enc_grad[None])


def solution(mesh):
    in_specs = (
        P("section", "dp", None, None),
        P("dp", None, None),
        P("dp", "section", None),
        P("dp", "section"),
        P("section", None),
        P("section", "dp", None),
        P("section", "dp", None),
        P("section", "dp", None),
        P("section", "dp", None),
    )
    out_specs = (P("section", "dp", None, None), P("dp", "section", None))

    def run(*args):
        per_device = head_device if plan_fits(mesh.shape, args[5].shape[2]) else relay_device
        return jax.shard_map(
            per_device, mesh=mesh, in_specs=in_specs, out_specs=out_specs, check_vma=False
        )(*args)

    return run
```

```python
import functools

import jax
import jax.numpy as jnp
from jax import lax
from jax.experimental import pallas as pl
from jax.experimental.pallas import tpu as pltpu
from jax.sharding import PartitionSpec as P

HEAD = 64


def from_behind(array, axis, by):
    length = lax.axis_size(axis)
    pairs = [(i, i + by) for i in range(length) if 0 <= i + by < length]
    return lax.ppermute(array, axis, pairs)


def times_transposed(left_side, right_side):
    return lax.dot_general(
        left_side, right_side, (((1,), (1,)), ((), ())), preferred_element_type=jnp.float32
    )


def project_keys(encoded, key_weight, value_weight):
    keys_all = jnp.dot(encoded, key_weight, preferred_element_type=jnp.float32).astype(jnp.bfloat16)
    values_all = jnp.dot(encoded, value_weight, preferred_element_type=jnp.float32).astype(
        jnp.bfloat16
    )
    return (keys_all, values_all)


def relay_device(
    hidden_in, grad_out, encoder_out, enc_valid, norm_gain, w_query, w_key, w_value, w_out
):
    section_count = lax.axis_size("section")
    my_section = lax.axis_index("section")
    valid_half = enc_valid.astype(jnp.bfloat16)
    encoded_all, valid_all = (
        lax.all_gather(encoder_out, "section", axis=1, tiled=True),
        lax.all_gather(valid_half, "section", axis=1, tiled=True),
    )
    encoded = encoded_all[0]
    valid_keys = valid_all[0].astype(jnp.float32)
    query_full, key_full, value_full, out_full = (
        lax.all_gather(w_query, "dp", axis=1, tiled=True),
        lax.all_gather(w_key, "dp", axis=1, tiled=True),
        lax.all_gather(w_value, "dp", axis=1, tiled=True),
        lax.all_gather(w_out, "dp", axis=1, tiled=True),
    )
    keys_all, values_all = project_keys(encoded, key_full[0], value_full[0])
    query_weight = query_full[0]
    key_weight = key_full[0]
    value_weight = value_full[0]
    out_weight = out_full[0]
    dec_rows, width = (hidden_in.shape[2], hidden_in.shape[3])
    enc_rows = encoded.shape[0]
    inner_width = query_weight.shape[1]
    head_count = inner_width // HEAD
    in_float = hidden_in[0, 0].astype(jnp.float32)
    gain_row = norm_gain[0].astype(jnp.float32)
    inv_rms = lax.rsqrt(jnp.mean(in_float * in_float, axis=1, keepdims=True) + 1e-06)
    normed = (in_float * inv_rms * gain_row).astype(jnp.bfloat16)
    queries = jnp.dot(normed, query_weight, preferred_element_type=jnp.float32).astype(jnp.bfloat16)
    query_heads = queries.reshape(dec_rows, head_count, HEAD)
    key_heads = keys_all.reshape(enc_rows, head_count, HEAD)
    value_heads = values_all.reshape(enc_rows, head_count, HEAD)
    scores = jnp.einsum("lhd,ehd->hle", query_heads, key_heads, preferred_element_type=jnp.float32)
    raw = jnp.exp(scores) * valid_keys[None, None, :]
    attn_prob = raw / jnp.sum(raw, axis=2, keepdims=True)
    prob_half = attn_prob.astype(jnp.bfloat16)

    def backward_step(grad_y):
        grad_attn = times_transposed(grad_y, out_weight).astype(jnp.bfloat16)
        attn_heads = grad_attn.reshape(dec_rows, head_count, HEAD)
        grad_prob = jnp.einsum(
            "lhd,ehd->hle", attn_heads, value_heads, preferred_element_type=jnp.float32
        )
        inner_sum = jnp.sum(attn_prob * grad_prob, axis=2, keepdims=True)
        grad_scores = (attn_prob * (grad_prob - inner_sum)).astype(jnp.bfloat16)
        grad_query = jnp.einsum(
            "hle,ehd->lhd", grad_scores, key_heads, preferred_element_type=jnp.float32
        ).astype(jnp.bfloat16)
        grad_key = jnp.einsum(
            "hle,lhd->ehd", grad_scores, query_heads, preferred_element_type=jnp.float32
        ).astype(jnp.bfloat16)
        grad_value = jnp.einsum(
            "hle,lhd->ehd", prob_half, attn_heads, preferred_element_type=jnp.float32
        ).astype(jnp.bfloat16)
        grad_normed = times_transposed(grad_query.reshape(dec_rows, inner_width), query_weight)
        scaled_grad = gain_row * grad_normed
        branch = inv_rms * scaled_grad - in_float * inv_rms * inv_rms * inv_rms * jnp.mean(
            in_float * scaled_grad, axis=1, keepdims=True
        )
        grad_input = (grad_y.astype(jnp.float32) + branch).astype(jnp.bfloat16)
        return (
            grad_input,
            grad_key.reshape(enc_rows, inner_width),
            grad_value.reshape(enc_rows, inner_width),
        )

    zero_input = jnp.zeros((dec_rows, width), jnp.bfloat16)
    zero_enc = jnp.zeros((enc_rows, inner_width), jnp.bfloat16)

    def loop_body(step_index, state_now):
        grad_now, grad_done, key_grad, value_grad = state_now
        is_active = my_section == section_count - 1 - step_index
        grad_done, key_grad, value_grad = lax.cond(
            is_active, lambda: backward_step(grad_now), lambda: (grad_done, key_grad, value_grad)
        )
        grad_now = from_behind(grad_done, "section", -1)
        return (grad_now, grad_done, key_grad, value_grad)

    grad_now, grad_done, key_grad, value_grad = lax.fori_loop(
        0, section_count - 1, loop_body, (grad_out[0], zero_input, zero_enc, zero_enc)
    )
    grad_done, key_grad, value_grad = lax.cond(
        my_section == 0, lambda: backward_step(grad_now), lambda: (grad_done, key_grad, value_grad)
    )
    enc_grad = lax.psum_scatter(
        (
            times_transposed(key_grad, key_weight) + times_transposed(value_grad, value_weight)
        ).astype(jnp.bfloat16),
        "section",
        scatter_dimension=0,
        tiled=True,
    )
    return (grad_done[None, None], enc_grad[None])

CORES = 2
ANY = pl.BlockSpec(memory_space=pl.ANY)
SMEM = pl.BlockSpec(memory_space=pltpu.SMEM)
VMEM = pl.BlockSpec(memory_space=pltpu.VMEM)
F32, BF16 = jnp.float32, jnp.bfloat16


def plan_fits(mesh_shape, dims):
    sections, ranks = mesh_shape["section"], mesh_shape["dp"]
    return sections == 4 and dims == ranks * sections * HEAD and ranks == 8


def dot_nt(a, b):
    return lax.dot_general(a, b, (((1,), (1,)), ((), ())), preferred_element_type=F32)


def dot_tn(a, b):
    return lax.dot_general(a, b, (((0,), (0,)), ((), ())), preferred_element_type=F32)


def dot_nn(a, b):
    return jnp.dot(a, b, preferred_element_type=F32)


def call(body, outs, inputs, specs, scratch, flops, size, out_specs=None, after=()):
    count = len(inputs)

    def kernel(*refs):
        body(*refs[:count], *refs[count + len(after) :])

    return list(pl.pallas_call(
        kernel,
        out_shape=outs,
        in_specs=specs + [ANY] * len(after),
        out_specs=[VMEM] * len(outs) if out_specs is None else out_specs,
        scratch_shapes=scratch,
        cost_estimate=pl.CostEstimate(flops=flops, bytes_accessed=size, transcendentals=0),
        compiler_params=pltpu.CompilerParams(vmem_limit_bytes=56 * 2**20),
    )(*inputs, *after))


def choose(sources, index, target, sem):
    if len(sources) == 1:
        copy = pltpu.make_async_copy(sources[0], target, sem)
        copy.start()
        return copy
    for i, source in enumerate(sources):

        @pl.when(index == i)
        def _(source=source):
            pltpu.make_async_copy(source, target, sem).start()

    return pltpu.make_async_copy(sources[0], target, sem)


def pieces_body(sections, half, me_ref, first_ref, second_ref, *rest):
    outs, buf, sems = rest[:sections], rest[sections], rest[sections + 1]
    me = me_ref[0]
    rows, inner = first_ref.shape
    part = inner // sections
    group = sections * HEAD
    lane = lax.broadcasted_iota(jnp.int32, (rows, 2 * HEAD), 1)
    waits = []
    for p in range(sections):
        for i, ref in enumerate((first_ref, second_ref) if half == 0 else (first_ref,)):
            for m in range(part // (2 * HEAD)):
                at = 2 * group * m + 2 * HEAD * (p // 2)
                low, high = ref[:, at : at + 2 * HEAD], ref[:, at + group : at + group + 2 * HEAD]
                if p % 2 == 0:
                    high = jnp.concatenate([high[:, HEAD:], high[:, :HEAD]], axis=1)
                else:
                    low = jnp.concatenate([low[:, HEAD:], low[:, :HEAD]], axis=1)
                to = part * i + 2 * HEAD * m
                buf[p, :, to : to + 2 * HEAD] = jnp.where(lane < HEAD, low, high)
        if half == 1:
            for i in range(sections):
                buf[p, HEAD * i : HEAD * (i + 1), part:] = second_ref[
                    HEAD * p : HEAD * (p + 1), part * i : part * (i + 1)
                ]
        for k in range(sections):

            @pl.when((me ^ k) == p)
            def _(k=k, p=p):
                pltpu.make_async_copy(buf.at[p], outs[k], sems.at[p]).start()

        waits.append(pltpu.make_async_copy(buf.at[p], outs[0], sems.at[p]))
    for w in waits:
        w.wait()


def pick_body(tables, me_ref, *refs):
    sources, (target, buf, sems) = refs[:-3], refs[-3:]
    width = sources[0].shape[1]
    copies = [
        choose(sources, lookup(table, me_ref[0]), buf.at[i], sems.at[i])
        for i, table in enumerate(tables)
    ]
    outs = []
    for i, copy in enumerate(copies):
        copy.wait()
        to = target.at[:, width * i : width * (i + 1)]
        outs.append(pltpu.make_async_copy(buf.at[i], to, sems.at[len(tables) + i]))
        outs[-1].start()
    for out in outs:
        out.wait()


def encoder_rows_body(sections, me_ref, *refs):
    packs, (enc, valid_out, gain_out) = refs[:sections], refs[sections:]
    me = me_ref[0]
    rows = enc.shape[0] // sections
    valid = jnp.zeros((1, enc.shape[0]), F32)
    for k in range(sections):
        enc[pl.ds(pl.multiple_of((me ^ k) * rows, rows), rows), :] = packs[k][:rows, :]
        tail = packs[k][rows : rows + 16, :].astype(F32)
        valid = valid + tail[0:1, : enc.shape[0]]
        gain_out[me ^ k] = jnp.broadcast_to(tail[1:2, :], gain_out.shape[1:])
    valid_out[...] = jnp.broadcast_to(valid, valid_out.shape)


def forward_body(sections, section, source, me_ref, *refs):
    xs, refs = refs[:sections], refs[sections:]
    enc, valid_ref, gain_ref, refs = refs[0], refs[1], refs[2], refs[3:]
    gs, refs = refs[: source.count], refs[source.count :]
    q_out, k_out, prob_out, x_rows, inv_rows, x_buf, w_buf, sems = refs
    me = me_ref[0]
    x_copy = choose(xs, me ^ section, x_buf, sems.at[0])
    part = q_out.shape[1]
    w_copies = [source.load(gs, me, i, part, w_buf.at[i], sems.at[1 + i]) for i in range(2)]
    gain, valid = gain_ref[section, 0:1, :], valid_ref[0:1, :]
    w_copies[1].wait()
    k_out[...] = dot_nn(enc[...], w_buf[1]).astype(BF16)
    x_copy.wait()
    x = x_buf[...].astype(F32)
    inv = lax.rsqrt(jnp.mean(x * x, axis=1, keepdims=True) + 1e-06)
    block = x_rows.shape[0]
    x_mine = x_buf[pl.ds(pl.multiple_of(me * block, block), block), :]
    x_rows[...] = x_mine
    mine = x_mine.astype(F32)
    inv_rows[...] = jnp.broadcast_to(
        lax.rsqrt(jnp.mean(mine * mine, axis=1, keepdims=True) + 1e-06), inv_rows.shape
    )
    x_buf[...] = (x * inv * gain).astype(BF16)
    w_copies[0].wait()
    q_out[...] = dot_nn(x_buf[...], w_buf[0]).astype(BF16)
    lane = lax.broadcasted_iota(jnp.int32, (q_out.shape[0], 2 * HEAD), 1)
    for pair in range(part // (2 * HEAD)):
        cols = slice(2 * HEAD * pair, 2 * HEAD * (pair + 1))
        q, k = q_out[:, cols], k_out[:, cols]
        for h in range(2):
            scores = dot_nt(jnp.where((lane < HEAD) == (h == 0), q, 0), k)
            raw = jnp.exp(scores) * valid
            prob_out[2 * pair + h] = (raw / jnp.sum(raw, axis=1, keepdims=True)).astype(BF16)


class Source:
    def __init__(self, arrays, places, table):
        self.arrays, self.places, self.table = arrays, places, table
        self.count = len(arrays)

    def load(self, refs, me, i, part, target, sem):
        views = [refs[a].at[:, part * (2 * h + i) : part * (2 * h + i + 1)] for a, h in self.places]
        return choose(views, lookup(self.table, me), target, sem)


def lookup(table, me):
    value = jnp.int32(table[0])
    for i in range(1, len(table)):
        value = jnp.where(me == i, jnp.int32(table[i]), value)
    return value


def chain_body(sections, first, second, whole, me_ref, *refs):
    grads, refs = (refs[:1], refs[1:]) if whole else (refs[:sections], refs[sections:])
    g1, refs = refs[: first.count], refs[first.count :]
    g2, refs = refs[: second.count], refs[second.count :]
    k_ref, enc, prob_ref = refs[:3]
    outs, refs = refs[3 : 3 + sections], refs[3 + sections :]
    score_out, attn_out, grad, v_ref, gq, total, w_buf, sems = refs
    me = me_ref[0]
    part = k_ref.shape[1]
    v_copy = second.load(g2, me, 0, part, w_buf.at[2], sems.at[2])
    o_copy = second.load(g2, me, 1, part, w_buf.at[0], sems.at[0])
    q_copy = first.load(g1, me, 0, part, w_buf.at[1], sems.at[1])
    block = total.shape[0] // sections
    if whole:
        grad = grads[0]
    else:
        rows_in = []
        for k in range(sections):
            to = grad.at[pl.ds(pl.multiple_of((me ^ k) * block, block), block), :]
            rows_in.append(pltpu.make_async_copy(grads[k], to, sems.at[3 + k]))
            rows_in[-1].start()
    v_copy.wait()
    v_ref[...] = dot_nn(enc[...], w_buf[2]).astype(BF16)
    if not whole:
        for copy in rows_in:
            copy.wait()
    o_copy.wait()
    ranks = part // HEAD
    attn = jnp.zeros((grad.shape[0], part), F32)
    for i in range(sections):
        weight = jnp.concatenate(
            [
                w_buf[0, (sections * r + i) * HEAD : (sections * r + i + 1) * HEAD, :]
                for r in range(ranks)
            ]
        )
        attn = attn + dot_nt(grad[:, part * i : part * (i + 1)], weight)
    attn_out[...] = attn.astype(BF16)
    lane = lax.broadcasted_iota(jnp.int32, (attn_out.shape[0], 2 * HEAD), 1)
    for pair in range(part // (2 * HEAD)):
        cols = slice(2 * HEAD * pair, 2 * HEAD * (pair + 1))
        a, v, k = attn_out[:, cols], v_ref[:, cols], k_ref[:, cols]
        got = []
        for h in range(2):
            grad_prob = dot_nt(jnp.where((lane < HEAD) == (h == 0), a, 0), v)
            prob = prob_ref[2 * pair + h].astype(F32)
            inner = jnp.sum(prob * grad_prob, axis=1, keepdims=True)
            score = (prob * (grad_prob - inner)).astype(BF16)
            score_out[2 * pair + h] = score
            got.append(dot_nn(score, k))
        gq[:, cols] = jnp.where(lane < HEAD, got[0], got[1]).astype(BF16)
    q_copy.wait()
    total[...] = dot_nt(gq[...], w_buf[1]).astype(BF16)
    for j in range(sections):
        outs[j][...] = total[pl.ds(pl.multiple_of((me ^ j) * block, block), block), :]


def encoder_body(sections, one, two, first, last, me_ref, *refs):
    g1, refs = refs[: one.count], refs[one.count :]
    g2, refs = refs[: two.count], refs[two.count :]
    score_ref, prob_ref, attn_ref, q_ref = refs[:4]
    refs = refs[4:]
    if not first:
        acc_in, refs = refs[0], refs[1:]
    if last:
        outs, refs = refs[:sections], refs[sections:]
    else:
        acc_out, refs = refs[0], refs[1:]
    gk, gv, total, w_buf, sems = refs
    me = me_ref[0]
    part = q_ref.shape[1]
    copies = [
        one.load(g1, me, 1, part, w_buf.at[0], sems.at[0]),
        two.load(g2, me, 0, part, w_buf.at[1], sems.at[1]),
    ]
    lane = lax.broadcasted_iota(jnp.int32, (q_ref.shape[0], 2 * HEAD), 1)

    @pl.loop(0, part // (2 * HEAD))
    def _(pair):
        cols = pl.ds(pl.multiple_of(2 * HEAD * pair, 2 * HEAD), 2 * HEAD)
        a, q = attn_ref[:, cols], q_ref[:, cols]
        ks = [dot_tn(score_ref[2 * pair + h], q) for h in range(2)]
        vs = [dot_tn(prob_ref[2 * pair + h], a) for h in range(2)]
        gk[:, cols] = jnp.where(lane < HEAD, ks[0], ks[1]).astype(BF16)
        gv[:, cols] = jnp.where(lane < HEAD, vs[0], vs[1]).astype(BF16)
    for c in copies:
        c.wait()
    value = dot_nt(gk[...], w_buf[0]) + dot_nt(gv[...], w_buf[1])
    if not first:
        value = value + acc_in[...]
    if not last:
        acc_out[...] = value
    else:
        total[...] = value.astype(BF16)
        block = total.shape[0] // sections
        for j in range(sections):
            outs[j][...] = total[pl.ds(pl.multiple_of((me ^ j) * block, block), block), :]


def finish_body(count, section, me_ref, *refs):
    terms, refs = refs[:4], refs[4:]
    grads, refs = refs[:count], refs[count:]
    x_ref, inv_ref, gain_ref, out = refs
    total = terms[0][...].astype(F32)
    for t in terms[1:]:
        total = total + t[...].astype(F32)
    scaled = gain_ref[section, 0:1, :] * total
    x, inv = x_ref[...].astype(F32), inv_ref[:, 0:1]
    branch = inv * scaled - x * inv * inv * inv * jnp.mean(x * scaled, axis=1, keepdims=True)
    block = out.shape[0]
    me = me_ref[0]
    if grads[0].shape[0] == block:
        grad = grads[0][...]
    else:
        grad = grads[0][pl.ds(pl.multiple_of(me * block, block), block), :]
    out[...] = (grad.astype(F32) + branch).astype(BF16)


def head_device(
    hidden_in, grad_out, encoder_out, enc_valid, norm_gain, w_query, w_key, w_value, w_out
):
    sections = lax.axis_size("section")
    ranks = lax.axis_size("dp")
    levels = ranks // CORES
    me = lax.axis_index("section")
    me_ref = jnp.reshape(me, (1,)).astype(jnp.int32)
    axes = ("section", "dp")
    shard, inner = w_query.shape[1], w_query.shape[2]
    width = hidden_in.shape[3]
    dec_rows = hidden_in.shape[2]
    enc_rows = encoder_out.shape[1]
    part = inner // sections
    heads = part // HEAD
    block = dec_rows // sections
    keys = enc_rows * sections

    def peer(array, k, targets):
        pairs = [((s ^ k) * ranks + r, s * ranks + r) for s in targets for r in range(ranks)]
        return lax.ppermute(array, axes, pairs)

    def peers(arrays, targets=range(sections)):
        return [arrays[0]] + [peer(arrays[k], k, targets) for k in range(1, sections)]

    def shape(dims, dtype=BF16):
        return jax.ShapeDtypeStruct(dims, dtype)

    def cut_pieces(half, first, second, after):
        return call(
            functools.partial(pieces_body, sections, half),
            [shape((shard, 2 * part))] * sections,
            [me_ref, first[0], second[0]],
            [SMEM, VMEM, VMEM],
            [pltpu.VMEM((sections, shard, 2 * part), BF16), pltpu.SemaphoreType.DMA((sections,))],
            0,
            4 * shard * inner * sections,
            out_specs=[ANY] * sections,
            after=after,
        )

    arrived = [peers(cut_pieces(0, w_query, w_key, []))]
    arrived.append(peers(cut_pieces(1, w_value, w_out, arrived[0][1:2])))
    valid_row = lax.dynamic_update_slice(
        jnp.zeros((1, width), BF16), enc_valid.astype(BF16), (0, me * enc_rows)
    )
    pack = jnp.concatenate([encoder_out[0], valid_row, norm_gain, jnp.zeros((14, width), BF16)])
    packs = peers([pack] * sections)
    hidden = peers([hidden_in[0, 0]] * sections)
    encoded, valid, gains = call(
        functools.partial(encoder_rows_body, sections),
        [shape((keys, width)), shape((8, keys), F32), shape((sections, 8, width), F32)],
        [me_ref] + packs,
        [SMEM] + [VMEM] * sections,
        [],
        0,
        4 * keys * width,
    )

    order = [
        [(i, 0)]
        + [(s, h) for s in reversed(range(sections)) for h in range(2) if (s, h) != (i, 0)]
        for i in range(sections)
    ]
    spans = [(0, 1), (1, 2 * sections - 3), (2 * sections - 3, 2 * sections - 1)]
    spans += [(2 * sections - 1, 2 * sections)]
    held = []
    for low, high in spans:
        wanted = [
            [(i ^ order[i][turn][0], order[i][turn][1]) for i in range(sections)]
            for turn in range(low, high)
        ]
        unique = sorted(set(sum(wanted, [])))
        options = [arrived[h][k] for k, h in unique]
        if len(options) > 1:
            tables = [[unique.index(w) for w in want] for want in wanted]
            value = call(
                functools.partial(pick_body, tables),
                [shape((shard, options[0].shape[1] * (high - low)))],
                [me_ref] + options,
                [SMEM] + [ANY] * len(options),
                [
                    pltpu.VMEM((high - low,) + options[0].shape, BF16),
                    pltpu.SemaphoreType.DMA((2 * (high - low),)),
                ],
                0,
                4 * options[0].size * (high - low),
                out_specs=[ANY],
            )[0]
        else:
            value = options[0]
        held.append(lax.all_gather(value, "dp", axis=0, tiled=True))
    place = {t: (j, t - low) for j, (low, high) in enumerate(spans) for t in range(low, high)}

    def source(s, h):
        found = [place[order[i].index((s, h))] for i in range(sections)]
        places = sorted(set(found))
        arrays = sorted({j for j, _ in places})
        return Source(
            [held[j] for j in arrays],
            [(arrays.index(j), at) for j, at in places],
            [places.index(f) for f in found],
        )

    gemm = 2 * dec_rows * width * part
    rows_spec = shape((block, width))
    halves = [(source(s, 0), source(s, 1)) for s in range(sections)]

    def forward(s, after):
        one = halves[s][0]
        return call(
            functools.partial(forward_body, sections, s, one),
            [shape((dec_rows, part)), shape((keys, part))]
            + [shape((heads, dec_rows, keys)), rows_spec, shape((block, 128), F32)],
            [me_ref] + hidden + [encoded, valid, gains] + one.arrays,
            [SMEM] + [ANY] * sections + [VMEM] * 3 + [ANY] * one.count,
            [
                pltpu.VMEM((dec_rows, width), BF16),
                pltpu.VMEM((2, width, part), BF16),
                pltpu.SemaphoreType.DMA((3,)),
            ],
            2 * gemm,
            8 * width * part,
            after=after,
        )

    def chain(s, grads, k, prob, after):
        one, two = halves[s]
        return call(
            functools.partial(chain_body, sections, one, two, len(grads) == 1),
            [rows_spec] * sections + [shape((heads, dec_rows, keys)), shape((dec_rows, part))],
            [me_ref] + grads + one.arrays + two.arrays + [k, encoded, prob],
            [SMEM]
            + [VMEM if len(grads) == 1 else ANY] * len(grads)
            + [ANY] * (one.count + two.count)
            + [VMEM] * 3,
            [
                pltpu.VMEM((dec_rows, width), BF16),
                pltpu.VMEM((keys, part), BF16),
                pltpu.VMEM((dec_rows, part), BF16),
                pltpu.VMEM((dec_rows, width), BF16),
                pltpu.VMEM((3, width, part), BF16),
                pltpu.SemaphoreType.DMA((3 + sections,)),
            ],
            3 * gemm,
            12 * width * part,
            after=after,
        )

    def encoder(s, score, prob, attn, q, acc, after):
        one, two = halves[s]
        return call(
            functools.partial(encoder_body, sections, one, two, not acc, s == 0),
            [shape((enc_rows, width))] * sections if s == 0 else [shape((keys, width), F32)],
            [me_ref] + one.arrays + two.arrays + [score, prob, attn, q] + acc,
            [SMEM] + [ANY] * (one.count + two.count) + [VMEM] * (4 + len(acc)),
            [
                pltpu.VMEM((keys, part), BF16),
                pltpu.VMEM((keys, part), BF16),
                pltpu.VMEM((keys, width), BF16),
                pltpu.VMEM((2, width, part), BF16),
                pltpu.SemaphoreType.DMA((2,)),
            ],
            2 * gemm,
            8 * width * part,
            after=after,
        )

    grads = [grad_out[0]]
    done, acc, ready = [None] * sections, [], None
    for s in reversed(range(sections)):
        q, k, prob, x_rows, inv_rows = forward(s, acc) if ready is None else ready
        ready = None
        outs = chain(s, grads, k, prob, acc)
        terms, score, attn = peers(outs[:sections]), outs[sections], outs[sections + 1]
        early = []
        if s in (1, sections - 1):
            ready = forward(s - 1, [attn])
            early = [ready[0]]
        if s == 0:
            acc = encoder(s, score, prob, attn, q, acc, [])
            early = [acc[0]]
        mine = call(
            functools.partial(finish_body, 1, s),
            [rows_spec],
            [me_ref] + terms + [grads[0], x_rows, inv_rows, gains],
            [SMEM] + [VMEM] * 8,
            [],
            block * width * 10,
            block * width * 20,
            after=early,
        )[0]
        grads = peers([mine] * sections, range(sections) if s > 0 else (0,))
        done[s] = grads
        if s > 0:
            acc = encoder(s, score, prob, attn, q, acc, [mine])
    enc_terms = peers(acc)

    def sum_body(*refs):
        total = refs[0][...].astype(F32)
        for r in refs[1:-1]:
            total = total + r[...].astype(F32)
        refs[-1][...] = total.astype(BF16)

    enc_grad = call(
        sum_body,
        [shape((enc_rows, width))],
        enc_terms,
        [VMEM] * sections,
        [],
        enc_rows * width * 4,
        enc_rows * width * 10,
    )[0]

    def result_body(me_ref, *refs):
        out, buf, sems = refs[-3:]
        me = me_ref[0]
        copies = [
            choose([refs[sections * s + k] for s in range(sections)], me, buf.at[k], sems.at[k])
            for k in range(sections)
        ]
        outs = []
        for k in range(sections):
            copies[k].wait()
            to = out.at[pl.ds(pl.multiple_of((me ^ k) * block, block), block)]
            outs.append(pltpu.make_async_copy(buf.at[k], to, sems.at[sections + k]))
            outs[-1].start()
        for copy in outs:
            copy.wait()

    result = call(
        result_body,
        [shape((dec_rows, width))],
        [me_ref] + [g for s in range(sections) for g in done[s]],
        [SMEM] + [ANY] * (sections * sections),
        [pltpu.VMEM((sections, block, width), BF16), pltpu.SemaphoreType.DMA((2 * sections,))],
        0,
        dec_rows * width * 4,
        out_specs=[ANY],
    )[0]
    return (result[None, None], enc_grad[None])


def solution(mesh):
    in_specs = (
        P("section", "dp", None, None),
        P("dp", None, None),
        P("dp", "section", None),
        P("dp", "section"),
        P("section", None),
        P("section", "dp", None),
        P("section", "dp", None),
        P("section", "dp", None),
        P("section", "dp", None),
    )
    out_specs = (P("section", "dp", None, None), P("dp", "section", None))

    def run(*args):
        per_device = head_device if plan_fits(mesh.shape, args[5].shape[2]) else relay_device
        return jax.shard_map(
            per_device, mesh=mesh, in_specs=in_specs, out_specs=out_specs, check_vma=False
        )(*args)

    return run
```
